32 devices in a mesh: seq: 8 (over z, y), head: 4 (over x, core).
Axes of the slice: x: 2, y: 2, z: 4, core: 2. Of those that a mesh axis runs over, the one named last changes fastest.
Arguments:
- tokens: bfloat16 [2048, 768], P('seq'), may hold values from -6 to 6
- cotangent: float32 [2048, 768], P('seq'), may hold values from -6 to 6
- doc_lengths: int32 [4], replicated, may hold values from 1 to 1024, 2048 in all
- norm_gain: float32 [2, 768], replicated, may hold values from 0.25 to 1.75
- gate_proj: bfloat16 [2, 768, 1536], P(None, None, 'head'), may hold values from -0.21875 to 0.21875
- value_proj: bfloat16 [2, 768, 1536], P(None, None, 'head'), may hold values from -0.21875 to 0.21875
- state_proj: bfloat16 [2, 768, 256], replicated, may hold values from -0.046875 to 0.046875
- step_proj: bfloat16 [2, 768, 24], P(None, None, 'head'), may hold values from -0.109375 to 0.109375
- step_bias: float32 [2, 24], P(None, 'head'), may hold values from -1.5 to 0.5
- decay_log: float32 [2, 24], P(None, 'head'), may hold values from -14 to -2.9
- skip_gain: float32 [2, 24], P(None, 'head'), may hold values from 0.5 to 2
- filter_value: float32 [2, 4, 1536], P(None, None, 'head'), may hold values from -3 to 3
- filter_value_bias: float32 [2, 1536], P(None, 'head'), may hold values from -3 to 3
- filter_state: float32 [2, 4, 256], replicated, may hold values from -3 to 3
- filter_state_bias: float32 [2, 256], replicated, may hold values from -1.5 to 1.5
- gated_gain: float32 [2, 1536], P(None, 'head'), may hold values from 0.25 to 1.75
- out_proj: bfloat16 [2, 1536, 768], P(None, 'head'), may hold values from -0.15625 to 0.15625
Outputs:
- mixed: bfloat16 [2048, 768], P('seq', 'head')
- grad_tokens: float32 [2048, 768], P('seq', 'head')
- grad_norm_gain: float32 [2, 768], P(None, 'head')
- grad_gate_proj: float32 [2, 768, 1536], P(None, 'seq', 'head')
- grad_value_proj: float32 [2, 768, 1536], P(None, 'seq', 'head')
- grad_state_proj: float32 [2, 768, 256], P(None, 'seq', 'head')
- grad_step_proj: float32 [2, 768, 24], P(None, 'seq', 'head')
- grad_step_bias: float32 [2, 24], P(None, 'head')
- grad_decay_log: float32 [2, 24], P(None, 'head')
- grad_skip_gain: float32 [2, 24], P(None, 'head')
- grad_filter_value: float32 [2, 4, 1536], P(None, None, 'head')
- grad_filter_value_bias: float32 [2, 1536], P(None, 'head')
- grad_filter_state: float32 [2, 4, 256], P(None, None, 'head')
- grad_filter_state_bias: float32 [2, 256], P(None, 'head')
- grad_gated_gain: float32 [2, 1536], P(None, 'head')
- grad_out_proj: float32 [2, 1536, 768], P(None, 'head', 'seq')
The draws below stay inside these ranges and needn't reach their ends.
All inputs are finite; a program needn't handle non-finite values.
Results may differ from the reference program's by a relative error of at most 0.017.
The reference program's roundings to bfloat16 on the way (of `normed`, `unit_rows`, `grad_rows` and `gate_low`) count: a program that leaves them out, or rounds other values in their place, can miss the bound.
Values may be sent and summed in bfloat16 or wider, within the bound.
No kernel may reach another device: no remote copies, remote signals or barrier semaphores. Data moves between devices by JAX's collectives and lax.ppermute only.
A program may use at most 128 MiB of HBM per device.

```python
import math
import jax
import jax.numpy as jnp
import numpy as np
from jax import lax

D = 768
HEADS = 24
HEADDIM = 64
STATE = 128
CONV = 4
GROUP = 256
LAYERS = 2
DOCS = 4
INNER = 1536
TOKENS = 2048


def draw_decay_log(key, part):
    lowest = math.log(0.1 / TOKENS)
    upper_rate = math.log(0.05)
    return jax.random.uniform(key, (LAYERS, HEADS), jnp.float32, lowest, upper_rate)


def strengthened(array, rng, source, target, shards_of, factor):
    owner, partner = [(jnp.arange(array.shape[dim]) // (array.shape[dim] // shards_of)).reshape([-1 if axis == dim else 1 for axis in range(array.ndim)]) for dim in (source, target)]
    chosen = jax.random.permutation(rng, shards_of)[partner]
    strong = (owner == chosen) | (owner == (partner + shards_of // 2) % shards_of)
    return jnp.where(strong, factor * array, array)


def block_levels(stream_key, dims, shards, smallest, largest):
    loudness = 1.0
    for axis_at, blocks in shards:
        heights = jax.random.uniform(jax.random.fold_in(jax.random.fold_in(stream_key, 6), axis_at), (blocks,), jnp.float32, smallest / len(shards), largest / len(shards))
        loudness = loudness * jnp.repeat(jnp.exp(heights), dims[axis_at] // blocks).reshape((-1,) + (1,) * (len(dims) - 1 - axis_at))
    return loudness


def split_up(count, total, bound, lean):
    loads = [(1 << 20) // math.isqrt(rank ** lean) + 1 for rank in range(2, count + 1)]
    rest, holding = total - bound - (count - 1), [1] * (count - 1)
    while rest > 0:
        candidates = [i for i in range(count - 1) if holding[i] < bound]
        pool, remaining = sum([loads[i] for i in candidates]), rest
        for i in candidates:
            more = min(bound - holding[i], max(1, remaining * loads[i] // pool), rest)
            holding[i] = holding[i] + more
            rest = rest - more
    return np.array([bound] + holding)


def ragged_sizes(own_key, number_of, total, bound, skew):
    if number_of == 2:
        one = jax.random.randint(own_key, (), max(1, total - bound), min(bound, total - 1) + 1)
        return jnp.stack([one, total - one])
    sizes = jnp.asarray(split_up(number_of, total, bound, skew), jnp.int32)
    twos = (number_of - 1) // 2
    giver, receiver = sizes[1:1 + 2 * twos:2], sizes[2:2 + 2 * twos:2]
    slack = jnp.minimum(giver - 1, bound - receiver)
    moved = jax.random.randint(jax.random.fold_in(own_key, 1), (twos,), 0, 1 << 20) % (slack + 1)
    sizes = sizes.at[1:1 + 2 * twos:2].set(giver - moved).at[2:2 + 2 * twos:2].set(receiver + moved)
    return sizes[jax.random.permutation(jax.random.fold_in(own_key, 2), number_of)]


def gaussian(key, dims, deviation, limit, shards=(), kind=jnp.bfloat16):
    result = jax.random.normal(key, dims, jnp.float32) * deviation
    if len(shards) > 0:
        result = block_levels(key, dims, shards, -0.22, 0.18) * result
    return jnp.clip(result, min=-limit, max=limit).astype(kind)


def noise_with(stream_key, extent, deviation, reach, cuts, heavy, kind=jnp.bfloat16):
    array = deviation * jax.random.normal(stream_key, extent, jnp.float32)
    if cuts:
        array = array * block_levels(stream_key, extent, cuts, -0.22, 0.18)
    return jnp.clip(strengthened(array, jax.random.fold_in(stream_key, 3), *heavy), -reach, reach).astype(kind)


def setup_inputs(seed: int = 0) -> dict:
    key_of = jax.random.split(jax.random.key(seed), 18)
    tokens = noise_with(key_of[0], (TOKENS, D), 1.0, 6.0, ((0, 8),), (0, 1, 8, 2.0))
    cotangent = gaussian(key_of[1], (TOKENS, D), 1.0, 6.0, ((0, 8),), jnp.float32)
    doc_lengths = ragged_sizes(key_of[2], DOCS, TOKENS, TOKENS // 2, 0).astype(jnp.int32)
    norm_gain = jnp.clip(1.0 + 0.15 * jax.random.normal(key_of[3], (LAYERS, D), jnp.float32), 0.25, 1.75)
    gate_proj = gaussian(key_of[4], (LAYERS, D, INNER), D ** -0.5, 0.21875, ((2, 4),))
    value_proj = gaussian(key_of[5], (LAYERS, D, INNER), D ** -0.5, 0.21875, ((2, 4),))
    state_proj = gaussian(key_of[6], (LAYERS, D, 2 * STATE), (25 * D) ** -0.5, 0.046875)
    step_proj = gaussian(key_of[7], (LAYERS, D, HEADS), (4 * D) ** -0.5, 0.109375, ((2, 4),))
    step_bias = jnp.clip(-1.5 + 2.0 * jax.random.uniform(key_of[8], (LAYERS, HEADS), jnp.float32) ** block_levels(key_of[8], (LAYERS, HEADS), ((1, 4),), -0.2, 0.2), -1.5, 0.5)
    decay_log = draw_decay_log(jax.random.fold_in(key_of[17], 71), 0)
    skip_gain = jnp.clip(0.5 + 1.5 * jax.random.uniform(key_of[10], (LAYERS, HEADS), jnp.float32) ** block_levels(key_of[10], (LAYERS, HEADS), ((1, 4),), -0.2, 0.2), 0.5, 2.0)
    filter_value = gaussian(key_of[11], (LAYERS, CONV, INNER), 0.5, 3.0, ((2, 4),), jnp.float32)
    filter_value_bias = gaussian(key_of[12], (LAYERS, INNER), 0.3, 3.0, ((1, 4),), jnp.float32)
    filter_state = gaussian(key_of[13], (LAYERS, CONV, 2 * STATE), 0.5, 3.0, (), jnp.float32)
    filter_state_bias = gaussian(key_of[14], (LAYERS, 2 * STATE), 0.1, 1.5, (), jnp.float32)
    gated_gain = jnp.clip(1.0 + 0.15 * jax.random.normal(key_of[15], (LAYERS, INNER), jnp.float32), 0.25, 1.75)
    out_proj = gaussian(key_of[16], (LAYERS, INNER, D), INNER ** -0.5, 0.15625, ((1, 4),))
    return {"tokens": tokens, "cotangent": cotangent, "doc_lengths": doc_lengths, "norm_gain": norm_gain, "gate_proj": gate_proj, "value_proj": value_proj, "state_proj": state_proj, "step_proj": step_proj, "step_bias": step_bias, "decay_log": decay_log, "skip_gain": skip_gain, "filter_value": filter_value, "filter_value_bias": filter_value_bias, "filter_state": filter_state, "filter_state_bias": filter_state_bias, "gated_gain": gated_gain, "out_proj": out_proj}


epsilon = 1e-05
highest = lax.Precision.HIGHEST

def segment_of(doc_lengths, positions):
    starts = jnp.cumsum(doc_lengths) - doc_lengths
    return lax.optimization_barrier(jnp.sum((positions[:, None] >= starts[None, :]).astype(jnp.int32), axis=1)) - 1

def short_filter(padded, weight, bias, seg_padded, segment):
    row_total = segment.shape[0]
    summed = jnp.zeros((row_total, padded.shape[1]), jnp.float32) + bias[None, :]
    for offset in range(CONV):
        start_row = CONV - 1 - offset
        shifted = padded[start_row:start_row + row_total]
        same_doc = (seg_padded[start_row:start_row + row_total] == segment).astype(jnp.float32)
        summed = summed + weight[offset][None, :] * shifted * same_doc[:, None]
    return summed

def silu_grad(pre):
    sigmoid_value = jax.nn.sigmoid(pre)
    return sigmoid_value * (1.0 + pre * (1.0 - sigmoid_value))

def block_step(values, steps, b_rows, c_rows, segment, before, decay_rate, state_in):
    row_total = segment.shape[0]
    log_steps = steps * decay_rate[None, :]
    cumulative = jnp.cumsum(log_steps, axis=0)
    position = jnp.arange(row_total, dtype=jnp.int32)
    allowed = (position[:, None] >= position[None, :]) & (segment[:, None] == segment[None, :])
    log_gap = cumulative[:, None, :] - cumulative[None, :, :]
    decays = jnp.where(allowed[:, :, None], jnp.exp(jnp.where(allowed[:, :, None], log_gap, 0.0)), 0.0)
    scores = jnp.dot(c_rows, b_rows.T, precision=highest)
    weights = decays * scores[:, :, None]
    stepped = steps[:, :, None] * values
    output = jnp.einsum('tsh,shp->thp', weights, stepped, precision=highest)
    entering = jnp.exp(cumulative) * (segment == before).astype(jnp.float32)[:, None]
    carried = jnp.einsum('tn,hpn->thp', c_rows, state_in, precision=highest)
    output = output + entering[:, :, None] * carried
    tail_gain = jnp.exp(cumulative[-1][None, :] - cumulative) * (segment == segment[-1]).astype(jnp.float32)[:, None] * steps
    through = jnp.exp(cumulative[-1]) * (segment[-1] == before).astype(jnp.float32)
    state_out = jnp.einsum('shp,sn->hpn', tail_gain[:, :, None] * values, b_rows, precision=highest) + through[:, None, None] * state_in
    return (output, state_out)

def scan_sequence(values, steps, b_rows, c_rows, segment, decay_rate):
    row_total = values.shape[0]
    blocks = row_total // GROUP
    head_total = values.shape[1]
    before = jnp.concatenate([jnp.full((1,), -1, jnp.int32), segment[GROUP - 1:row_total - 1:GROUP].astype(jnp.int32)])
    items = (values.reshape(blocks, GROUP, head_total, HEADDIM), steps.reshape(blocks, GROUP, head_total), b_rows.reshape(blocks, GROUP, STATE), c_rows.reshape(blocks, GROUP, STATE), segment.reshape(blocks, GROUP), before)

    def advance(state, item):
        output, state_next = block_step(item[0], item[1], item[2], item[3], item[4], item[5], decay_rate, state)
        return (state_next, output)
    start_state = jnp.zeros((head_total, HEADDIM, STATE), jnp.float32)
    _, outputs = lax.scan(jax.checkpoint(advance), start_state, items)
    return outputs.reshape(row_total, head_total, HEADDIM)

def contract_first(left, right, exact):
    if exact:
        return lax.dot_general(left, right, (((0,), (0,)), ((), ())), precision=highest, preferred_element_type=jnp.float32)
    return lax.dot_general(left, right, (((0,), (0,)), ((), ())), preferred_element_type=jnp.float32)

def contract_last(left, right, exact):
    if exact:
        return lax.dot_general(left, right, (((1,), (1,)), ((), ())), precision=highest, preferred_element_type=jnp.float32)
    return lax.dot_general(left, right, (((1,), (1,)), ((), ())), preferred_element_type=jnp.float32)

def reference(tokens, cotangent, doc_lengths, norm_gain, gate_proj, value_proj, state_proj, step_proj, step_bias, decay_log, skip_gain, filter_value, filter_value_bias, filter_state, filter_state_bias, gated_gain, out_proj):
    row_total = tokens.shape[0]
    positions = jnp.arange(-(CONV - 1), row_total, dtype=jnp.int32)
    seg_padded = segment_of(doc_lengths, positions)
    segment = seg_padded[CONV - 1:]
    stream = tokens.astype(jnp.float32)
    stored = []
    for layer_index in range(LAYERS):
        row_scale = lax.rsqrt(lax.optimization_barrier(jnp.mean(stream * stream, axis=1)) + epsilon)
        normed = (stream * row_scale[:, None] * norm_gain[layer_index][None, :]).astype(jnp.bfloat16)
        gate_pre = jnp.dot(normed, gate_proj[layer_index], preferred_element_type=jnp.float32)
        value_pre = jnp.dot(normed, value_proj[layer_index], preferred_element_type=jnp.float32)
        state_pre = jnp.dot(normed, state_proj[layer_index], preferred_element_type=jnp.float32)
        step_raw = jnp.dot(normed, step_proj[layer_index], preferred_element_type=jnp.float32)
        joined = jnp.concatenate([value_pre, state_pre], axis=1)
        padded = jnp.concatenate([jnp.zeros((CONV - 1, joined.shape[1]), jnp.float32), joined], axis=0)
        filter_weight = jnp.concatenate([filter_value[layer_index], filter_state[layer_index]], axis=1)
        filter_bias = jnp.concatenate([filter_value_bias[layer_index], filter_state_bias[layer_index]], axis=0)
        filter_pre = short_filter(padded, filter_weight, filter_bias, seg_padded, segment)
        active = jax.nn.silu(filter_pre)
        values = active[:, :INNER].reshape(row_total, HEADS, HEADDIM)
        b_rows = active[:, INNER:INNER + STATE]
        c_rows = active[:, INNER + STATE:]
        step_pre = step_raw + step_bias[layer_index][None, :]
        steps = jax.nn.softplus(step_pre)
        decay_rate = -jnp.exp(decay_log[layer_index])
        scanned = scan_sequence(values, steps, b_rows, c_rows, segment, decay_rate)
        mixed_pre = (scanned + skip_gain[layer_index][None, :, None] * values).reshape(row_total, INNER)
        gated = mixed_pre * jax.nn.silu(gate_pre)
        gate_scale = lax.rsqrt(lax.optimization_barrier(jnp.mean(gated * gated, axis=1)) + epsilon)
        unit_rows = (gated * gate_scale[:, None] * gated_gain[layer_index][None, :]).astype(jnp.bfloat16)
        branch = jnp.dot(unit_rows, out_proj[layer_index], preferred_element_type=jnp.float32)
        stored.append((stream, row_scale, normed, gate_pre, padded, filter_weight, filter_bias, filter_pre, values, b_rows, c_rows, step_pre, steps, decay_rate, mixed_pre, gated, gate_scale, unit_rows))
        stream = stream + branch
    mixed = stream.astype(jnp.bfloat16)
    residual = cotangent
    gradients = [[None] * LAYERS for _ in range(15)]
    for layer_index in reversed(range(LAYERS)):
        stream_in, row_scale, normed, gate_pre, padded, filter_weight, filter_bias, filter_pre, values, b_rows, c_rows, step_pre, steps, decay_rate, mixed_pre, gated, gate_scale, unit_rows = stored[layer_index]
        grad_rows = residual.astype(jnp.bfloat16)
        unit_grad = contract_last(grad_rows, out_proj[layer_index], False)
        grad_out = contract_first(unit_rows, grad_rows, False)
        scaled = gated_gain[layer_index][None, :] * unit_grad
        inner_sum = lax.optimization_barrier(jnp.sum(scaled * gated, axis=1))
        scale_cube = gate_scale * gate_scale * gate_scale
        gated_grad = gate_scale[:, None] * scaled - gated * (scale_cube * inner_sum / INNER)[:, None]
        grad_gain_inner = lax.optimization_barrier(jnp.sum(unit_grad * gated * gate_scale[:, None], axis=0))
        mixed_grad = gated_grad * jax.nn.silu(gate_pre)
        gate_grad = gated_grad * mixed_pre * silu_grad(gate_pre)
        head_grad = mixed_grad.reshape(row_total, HEADS, HEADDIM)
        grad_skip = lax.optimization_barrier(jnp.sum(head_grad * values, axis=(0, 2)))
        _, pull_scan = jax.vjp(lambda a, b, c, d, e: scan_sequence(a, b, c, d, segment, e), values, steps, b_rows, c_rows, decay_rate)
        value_grad, step_grad, b_grad, c_grad, rate_grad = pull_scan(head_grad)
        value_grad = value_grad + head_grad * skip_gain[layer_index][None, :, None]
        grad_decay = rate_grad * decay_rate
        step_grad = step_grad * jax.nn.sigmoid(step_pre)
        grad_bias = lax.optimization_barrier(jnp.sum(step_grad, axis=0))
        active_grad = jnp.concatenate([value_grad.reshape(row_total, INNER), b_grad, c_grad], axis=1) * silu_grad(filter_pre)
        _, pull_filter = jax.vjp(lambda p, w, b: short_filter(p, w, b, seg_padded, segment), padded, filter_weight, filter_bias)
        padded_grad, weight_grad, bias_grad = pull_filter(active_grad)
        joined_grad = padded_grad[CONV - 1:]
        value_low = joined_grad[:, :INNER].astype(jnp.bfloat16)
        state_grad = joined_grad[:, INNER:]
        gate_low = gate_grad.astype(jnp.bfloat16)
        step_low = step_grad.astype(jnp.bfloat16)
        normed_single = normed.astype(jnp.float32)
        grad_gate = contract_first(normed, gate_low, False)
        grad_value = contract_first(normed, value_low, False)
        grad_step = contract_first(normed, step_low, False)
        grad_state = contract_first(normed_single, state_grad, True)
        normed_grad = contract_last(gate_low, gate_proj[layer_index], False) + contract_last(value_low, value_proj[layer_index], False) + contract_last(step_low, step_proj[layer_index], False) + contract_last(state_grad, state_proj[layer_index].astype(jnp.float32), True)
        norm_rows = stream_in * row_scale[:, None]
        mean_dot = lax.optimization_barrier(jnp.mean(normed_single * normed_grad, axis=1))
        grad_norm = lax.optimization_barrier(jnp.sum(normed_grad * norm_rows, axis=0))
        residual = residual + row_scale[:, None] * (norm_gain[layer_index][None, :] * normed_grad - norm_rows * mean_dot[:, None])
        found = (grad_norm, grad_gate, grad_value, grad_state, grad_step, grad_bias, grad_decay, grad_skip, weight_grad[:, :INNER], bias_grad[:INNER], weight_grad[:, INNER:], bias_grad[INNER:], grad_gain_inner, grad_out, grad_out)
        for which in range(15):
            gradients[which][layer_index] = found[which]
    stacked = [jnp.stack(gradients[which], axis=0) for which in range(14)]
    return (mixed, residual, stacked[0], stacked[1], stacked[2], stacked[3], stacked[4], stacked[5], stacked[6], stacked[7], stacked[8], stacked[9], stacked[10], stacked[11], stacked[12], stacked[13])
```

```python
import functools

import jax
import jax.numpy as jnp
from jax import lax
from jax.experimental import pallas as pl
from jax.experimental.pallas import tpu as pltpu
from jax.sharding import PartitionSpec as P

D = 768
HEADDIM = 64
STATE = 128
CONV = 4
LAYERS = 2
INNER = 1536
LANES = 128
EDGE = 8

epsilon = 1e-05
highest = lax.Precision.HIGHEST
high = lax.Precision.HIGH
f32 = jnp.float32
bf16 = jnp.bfloat16


def shifted(value, axis, by):
    count = lax.axis_size(axis)
    pairs = [(i, i + by) for i in range(count) if 0 <= i + by < count]
    return lax.ppermute(value, axis, pairs)


def partner(value, axis, mask):
    count = lax.axis_size(axis)
    return lax.ppermute(value, axis, [(i, i ^ mask) for i in range(count)])


def copies_over(value, axis):
    return [value] + [partner(value, axis, k) for k in range(1, lax.axis_size(axis))]


def butterfly_sum(value, axis):
    mask = 1
    while mask < lax.axis_size(axis):
        value = value + partner(value, axis, mask)
        mask *= 2
    return value


def scatter_sum(value, axis):
    count, here = lax.axis_size(axis), lax.axis_index(axis)
    bits = count.bit_length() - 1
    tail = value.shape[1:]
    value = value.reshape((2,) * bits + tail)
    for bit in range(bits):
        dim = bits - 1 - bit
        mine = (here >> bit) & 1
        keep = lax.dynamic_index_in_dim(value, mine, dim, keepdims=False)
        give = lax.dynamic_index_in_dim(value, 1 - mine, dim, keepdims=False)
        value = keep + partner(give, axis, 1 << bit)
    return value


def prefix(packed, sign, rows):
    count = lax.axis_size("seq")
    heads = rows // HEADDIM

    def split(part):
        return part[rows, :heads], part[:rows].reshape(heads, HEADDIM, STATE)

    def join(decay, state):
        tail = jnp.broadcast_to(jnp.pad(decay, (0, LANES - heads))[None, :], (EDGE, LANES))
        return jnp.concatenate([state.reshape(rows, STATE), tail], axis=0)

    before = None
    span = 1
    while span < count:
        own_decay, own_state = split(packed)
        far = [split(shifted(packed, "seq", sign * k * span)) for k in range(1, 4) if k * span < count]
        decay, state = far[-1]
        for near_decay, near_state in far[-2::-1]:
            state = near_state + near_decay[:, None, None] * state
            decay = decay * near_decay
        if before is None:
            total = (decay, state)
        else:
            total = (before[0] * decay, before[1] + before[0][:, None, None] * state)
        if span * 4 < count:
            packed = join(own_decay * decay, own_state + own_decay[:, None, None] * state)
        before = total
        span *= 4
    return before[1].reshape(rows, STATE)


def call(kernel, outs, name):
    return pl.pallas_call(
        kernel,
        out_shape=[jax.ShapeDtypeStruct(s, d) for s, d in outs],
        name=name,
        compiler_params=pltpu.CompilerParams(vmem_limit_bytes=56 * 1024 * 1024),
    )


def dot(a, b, precision=None):
    return lax.dot_general(a, b, (((1,), (0,)), ((), ())), precision=precision, preferred_element_type=f32)


def dot_last(a, b, precision=None):
    return lax.dot_general(a, b, (((1,), (1,)), ((), ())), precision=precision, preferred_element_type=f32)


def dot_first(a, b, precision=None):
    return lax.dot_general(a, b, (((0,), (0,)), ((), ())), precision=precision, preferred_element_type=f32)


def row_sums(x):
    return dot_last(jnp.ones((8, x.shape[1]), f32), x, highest)


def head_picker(rows):
    i = lax.broadcasted_iota(jnp.int32, (rows, LANES), 0)
    lane = lax.broadcasted_iota(jnp.int32, (rows, LANES), 1)
    return ((i >= lane * HEADDIM) & (i < (lane + 1) * HEADDIM)).astype(f32)


def spread(ref, columns, rows, heads):
    for k in range(heads):
        ref[:, k * HEADDIM : (k + 1) * HEADDIM] = jnp.broadcast_to(columns[:, k : k + 1], (rows, HEADDIM))
    return ref[...]


def silu(x):
    return x * jax.nn.sigmoid(x)


def silu_grad(x):
    s = jax.nn.sigmoid(x)
    return s * (1.0 + x * (1.0 - s))


def allowed_pairs(marks, seg_row, rows):
    i = lax.broadcasted_iota(jnp.int32, (rows, rows), 0)
    j = lax.broadcasted_iota(jnp.int32, (rows, rows), 1)
    return (i >= j) & (marks[:, 6:7] == seg_row[0:1, :])


def decays_of(cum, cum_t, allowed, k):
    gap = cum[:, k : k + 1] - cum_t[k : k + 1, :]
    return jnp.where(allowed, jnp.exp(jnp.where(allowed, gap, 0.0)), 0.0)


def scan_kernel(
    normed, edge, gate_w, value_w, state_w, step_w, filt, filt_bias, step_bias, rate, skip, marks, seg_row,
    gate_pre, joined, filter_pre, mixed_part, packed, step_pre, steps_out, cum_out,
    tail_scr, step_scr, *, heads,
):
    rows = normed.shape[0]
    x = normed[...]
    e = edge[...]
    marks = marks[...]
    joined[EDGE:, : 2 * STATE] = dot(x, state_w[...])
    joined[EDGE:, 2 * STATE :] = dot(x, value_w[...])
    joined[:EDGE, : 2 * STATE] = dot(e, state_w[...])[EDGE:]
    joined[:EDGE, 2 * STATE :] = dot(e, value_w[...])[EDGE:]
    pre_step = dot(x, step_w[...]) + step_bias[...]
    gate_pre[...] = dot(x, gate_w[...])
    pre = filt_bias[...] + filt[0:1, :] * joined[EDGE:, :]
    for k in range(1, CONV):
        pre = pre + filt[k : k + 1, :] * joined[EDGE - k : EDGE - k + rows, :] * marks[:, k : k + 1]
    filter_pre[...] = pre
    active = silu(pre)
    b = active[:, :STATE]
    c = active[:, STATE : 2 * STATE]
    values = active[:, 2 * STATE :]
    steps = jnp.maximum(pre_step, 0.0) + jnp.log1p(jnp.exp(-jnp.abs(pre_step)))
    i = lax.broadcasted_iota(jnp.int32, (rows, rows), 0)
    j = lax.broadcasted_iota(jnp.int32, (rows, rows), 1)
    cum = dot((i >= j).astype(f32), steps * rate[...], highest)
    step_pre[...] = pre_step
    steps_out[...] = steps
    cum_out[...] = cum
    cum_t = cum.T
    last = cum[rows - 1 : rows, :]
    tail = jnp.exp(last - cum) * marks[:, 5:6] * steps
    stepped = spread(step_scr, steps, rows, heads) * values
    packed[: heads * HEADDIM, :] = dot_first(spread(tail_scr, tail, rows, heads) * values, b, high)
    packed[heads * HEADDIM :, :] = jnp.broadcast_to(jnp.exp(last) * marks[0:1, 7:8], (EDGE, LANES))
    step_scr[...] = stepped
    tail_scr[...] = skip[...] * values
    scores = dot_last(c, b, high)
    allowed = allowed_pairs(marks, seg_row[...], rows)
    for k in range(heads):
        at = slice(k * HEADDIM, (k + 1) * HEADDIM)
        weights = scores * decays_of(cum, cum_t, allowed, k)
        mixed_part[:, at] = dot(weights, step_scr[:, at], high) + tail_scr[:, at]


def gate_kernel(mixed_part, filter_pre, gate_pre, cum, state_in, marks, mixed_pre, gated, squares, scr, *, heads):
    rows = mixed_part.shape[0]
    c = silu(filter_pre[:, STATE : 2 * STATE])
    carried = dot_last(c, state_in[...], high)
    entering = spread(scr, jnp.exp(cum[...]) * marks[:, 4:5], rows, heads)
    mixed = mixed_part[...] + entering * carried
    mixed_pre[...] = mixed
    out = mixed * silu(gate_pre[...])
    gated[...] = out
    squares[...] = row_sums(out * out)


def out_kernel(gated, gain, out_w, *refs):
    parts, (unit, branch, scale_row) = refs[:-3], refs[-3:]
    total = parts[0][...]
    for part in parts[1:]:
        total = total + part[...]
    scale = lax.rsqrt(total / INNER + epsilon)
    scale_row[...] = scale
    column = scale.T[:, 0:1]
    rows = (gated[...] * column * gain[...]).astype(bf16)
    unit[...] = rows
    branch[...] = dot(rows, out_w[...])


def unit_kernel(grad_rows, out_w, gain, gated, unit_grad, inner):
    grad = dot_last(grad_rows[...], out_w[...])
    unit_grad[...] = grad
    inner[...] = row_sums(gain[...] * grad * gated[...])


def gated_kernel(
    unit_grad, gated, gate_pre, mixed_pre, gain, scale_row, filter_pre, cum, marks, *refs, heads
):
    parts = refs[:-5]
    mixed_grad, gate_low, packed, row_out, scr = refs[-5:]
    rows = gated.shape[0]
    total = parts[0][...]
    for part in parts[1:]:
        total = total + part[...]
    scale = scale_row[...]
    cube = (scale * scale * scale * total / INNER).T[:, 0:1]
    column = scale.T[:, 0:1]
    grad = unit_grad[...]
    kept = gated[...]
    gated_grad = column * (gain[...] * grad) - kept * cube
    pre = gate_pre[...]
    mixed = gated_grad * silu(pre)
    mixed_grad[...] = mixed
    gate_low[...] = (gated_grad * mixed_pre[...] * silu_grad(pre)).astype(bf16)
    row_out[...] = jnp.zeros(row_out.shape, f32)
    row_out[0:1, :] = jnp.sum(grad * kept * column, axis=0, keepdims=True)
    values = silu(filter_pre[:, 2 * STATE :])
    row_out[1:2, :] = jnp.sum(mixed * values, axis=0, keepdims=True)
    c = silu(filter_pre[:, STATE : 2 * STATE])
    cum = cum[...]
    marks = marks[...]
    entering = spread(scr, jnp.exp(cum) * marks[:, 4:5], rows, heads)
    packed[: heads * HEADDIM, :] = dot_first(mixed * entering, c, high)
    packed[heads * HEADDIM :, :] = jnp.broadcast_to(
        jnp.exp(cum[rows - 1 : rows, :]) * marks[0:1, 7:8], (EDGE, LANES)
    )


def scan_grad_kernel(
    mixed_grad, filter_pre, mixed_pre, cum, steps, state_in, skip, marks, seg_row,
    stepped_grad, b_grad, c_grad, out_dot, full_scr, step_scr, *, heads,
):
    rows = mixed_grad.shape[0]
    marks = marks[...]
    active = silu(filter_pre[...])
    b = active[:, :STATE]
    c = active[:, STATE : 2 * STATE]
    values = active[:, 2 * STATE :]
    cum = cum[...]
    cum_t = cum.T
    grad = mixed_grad[...]
    entering = spread(full_scr, jnp.exp(cum) * marks[:, 4:5], rows, heads)
    direct = dot(grad * entering, state_in[...], high)
    out_dot[...] = dot(grad * (mixed_pre[...] - skip[...] * values), head_picker(heads * HEADDIM), highest)
    stepped = spread(step_scr, steps[...], rows, heads) * values
    step_scr[...] = stepped
    scores = dot_last(c, b, high)
    allowed = allowed_pairs(marks, seg_row[...], rows)
    score_grad = jnp.zeros((rows, rows), f32)
    for k in range(heads):
        at = slice(k * HEADDIM, (k + 1) * HEADDIM)
        decays = decays_of(cum, cum_t, allowed, k)
        own = mixed_grad[:, at]
        score_grad = score_grad + decays * dot_last(own, step_scr[:, at], high)
        stepped_grad[:, at] = dot_first(scores * decays, own, high)
    c_grad[...] = dot(score_grad, b, high) + direct
    b_grad[...] = dot_first(score_grad, c, high)


def filter_grad_kernel(
    later, packed, state_in, stepped_grad, b_grad, c_grad, out_dot, mixed_grad, filter_pre, joined, cum, steps,
    step_pre, rate, skip, marks, marks_ahead, filt,
    joined_grad, step_low, row_out, tail_scr, step_scr, pad_scr, state_scr, *, heads,
):
    rows = mixed_grad.shape[0]
    inner = heads * HEADDIM
    marks = marks[...]
    pre = filter_pre[...]
    active = silu(pre)
    b = active[:, :STATE]
    values = active[:, 2 * STATE :]
    cum = cum[...]
    step = steps[...]
    last = cum[rows - 1 : rows, :]
    tail = jnp.exp(last - cum) * marks[:, 5:6]
    ahead = later[...]
    tail_full = spread(tail_scr, tail, rows, heads)
    step_full = spread(step_scr, step, rows, heads)
    total = stepped_grad[...] + tail_full * dot_last(b, ahead, high)
    value_grad = step_full * total + skip[...] * mixed_grad[...]
    b_total = b_grad[...] + dot(tail_full * step_full * values, ahead, high)
    picker = head_picker(inner)
    step_direct = dot(total * values, picker, highest)
    through = jnp.exp(last) * marks[0:1, 7:8]
    for k in range(heads):
        at = slice(k * HEADDIM, (k + 1) * HEADDIM)
        state_scr[at, :] = ahead[at, :] * (
            packed[at, :] + jnp.broadcast_to(through[:, k : k + 1], (HEADDIM, STATE)) * state_in[at, :]
        )
    end = dot(row_sums(state_scr[...]), picker, highest)[0:1, :]
    i = lax.broadcasted_iota(jnp.int32, (rows, rows), 0)
    j = lax.broadcasted_iota(jnp.int32, (rows, rows), 1)
    log_grad = dot((i <= j).astype(f32), out_dot[...] - step * step_direct, highest) + end
    step_grad = (step_direct + rate[...] * log_grad) * jax.nn.sigmoid(step_pre[...])
    step_low[...] = step_grad.astype(bf16)
    slope = silu_grad(pre)
    width = pad_scr.shape[1]
    pad_scr[:EDGE, :] = jnp.zeros((EDGE, width), f32)
    pad_scr[EDGE + rows :, :] = jnp.zeros((EDGE, width), f32)
    pad_scr[EDGE : EDGE + rows, :STATE] = b_total * slope[:, :STATE]
    pad_scr[EDGE : EDGE + rows, STATE : 2 * STATE] = c_grad[...] * slope[:, STATE : 2 * STATE]
    pad_scr[EDGE : EDGE + rows, 2 * STATE :] = value_grad * slope[:, 2 * STATE :]
    grad = filt[0:1, :] * pad_scr[: EDGE + rows, :]
    for k in range(1, CONV):
        grad = grad + filt[k : k + 1, :] * pad_scr[k : k + EDGE + rows, :] * marks_ahead[:, k : k + 1]
    joined_grad[...] = grad
    own = pad_scr[EDGE : EDGE + rows, :]
    row_out[...] = jnp.zeros(row_out.shape, f32)
    for k in range(CONV):
        masked = own * joined[EDGE - k : EDGE - k + rows, :]
        if k > 0:
            masked = masked * marks[:, k : k + 1]
        row_out[k : k + 1, :] = jnp.sum(masked, axis=0, keepdims=True)
    row_out[4:5, :] = jnp.sum(own, axis=0, keepdims=True)
    row_out[5:6, :LANES] = jnp.sum(step_grad, axis=0, keepdims=True)
    row_out[6:7, :LANES] = jnp.sum(step * log_grad, axis=0, keepdims=True) * rate[...]


def normed_grad_kernel(
    joined_grad, edge_grad, gate_low, step_low, normed, gate_w, value_w, state_w, step_w,
    normed_part, dots, value_low, state_grad, scr,
):
    rows = normed.shape[0]
    scr[...] = joined_grad[EDGE:, :]
    scr[rows - EDGE :, :] = scr[rows - EDGE :, :] + edge_grad[...]
    low = scr[:, 2 * STATE :].astype(bf16)
    value_low[...] = low
    state = scr[:, : 2 * STATE]
    state_grad[...] = state
    part = (
        dot_last(gate_low[...], gate_w[...])
        + dot_last(low, value_w[...])
        + dot_last(step_low[...], step_w[...])
        + dot_last(state, state_w[...].astype(f32), high)
    )
    normed_part[...] = part
    dots[...] = row_sums(normed[...].astype(f32) * part)


def body(
    tokens,
    cotangent,
    doc_lengths,
    norm_gain,
    gate_proj,
    value_proj,
    state_proj,
    step_proj,
    step_bias,
    decay_log,
    skip_gain,
    filter_value,
    filter_value_bias,
    filter_state,
    filter_state_bias,
    gated_gain,
    out_proj,
):
    rows = tokens.shape[0]
    head_count = lax.axis_size("head")
    seq_count = lax.axis_size("seq")
    me = lax.axis_index("head")
    inner = gate_proj.shape[2]
    heads = step_proj.shape[2]
    width = 2 * STATE + inner
    share = D // head_count
    part_rows = rows // head_count
    state_share = 2 * STATE // head_count

    def columns(matrix):
        return lax.dynamic_slice_in_dim(matrix, me * share, share, matrix.ndim - 1)

    def own_rows(matrix):
        return lax.dynamic_slice_in_dim(matrix, me * part_rows, part_rows, 0)

    def to_columns(matrix):
        blocks = matrix.reshape(part_rows, head_count, share).transpose(1, 0, 2)
        return lax.all_to_all(blocks, "head", 0, 0, tiled=True).reshape(rows, share)

    positions = lax.axis_index("seq") * rows + jnp.arange(-EDGE, rows + EDGE, dtype=jnp.int32)
    starts = jnp.cumsum(doc_lengths) - doc_lengths
    documents = jnp.sum((positions[:, None] >= starts[None, :]).astype(jnp.int32), axis=1) - 1
    segment = documents[EDGE : EDGE + rows]
    before = documents[EDGE - 1]

    def same(offset):
        return (documents[EDGE - offset : EDGE - offset + rows] == segment).astype(f32)

    marks = jnp.stack(
        [
            same(0),
            same(1),
            same(2),
            same(3),
            (segment == before).astype(f32),
            (segment == segment[-1]).astype(f32),
            segment.astype(f32),
            jnp.broadcast_to((segment[-1] == before).astype(f32), (rows,)),
        ],
        axis=1,
    )
    seg_row = jnp.broadcast_to(segment.astype(f32)[None, :], (8, rows))
    ahead = [
        (documents[k : k + EDGE + rows] == documents[: EDGE + rows]).astype(f32) for k in range(CONV)
    ]
    marks_ahead = jnp.stack(ahead + ahead, axis=1)

    def lanes(vector):
        return jnp.pad(vector, (0, LANES - heads))[None, :]

    def layer_weights(l):
        return dict(
            gate=gate_proj[l],
            value=value_proj[l],
            state=state_proj[l],
            step=jnp.pad(step_proj[l], ((0, 0), (0, LANES - heads))),
            filt=jnp.concatenate([filter_state[l], filter_value[l]], axis=1),
            filt_bias=jnp.concatenate([filter_state_bias[l], filter_value_bias[l]])[None, :],
            bias=lanes(step_bias[l]),
            rate=lanes(-jnp.exp(decay_log[l])),
            skip=jnp.repeat(skip_gain[l], HEADDIM)[None, :],
            gain=gated_gain[l][None, :],
            out=out_proj[l],
        )

    weights = [layer_weights(l) for l in range(LAYERS)]
    vmem = pltpu.VMEM

    def with_scratch(kernel, outs, name, scratch):
        return pl.pallas_call(
            kernel,
            out_shape=[jax.ShapeDtypeStruct(s, d) for s, d in outs],
            scratch_shapes=[vmem(s, f32) for s in scratch],
            name=name,
            compiler_params=pltpu.CompilerParams(vmem_limit_bytes=56 * 1024 * 1024),
        )

    kept = []
    full = tokens.astype(f32)
    scale_full = lax.rsqrt(jnp.mean(full * full, axis=1) + epsilon)
    normed = (full * scale_full[:, None] * norm_gain[0][None, :]).astype(bf16)
    stream_rows = own_rows(full)
    stream_columns = columns(full)
    scale_rows = own_rows(scale_full)
    mixed = None
    for l in range(LAYERS):
        w = weights[l]
        edge = shifted(normed[rows - 2 * EDGE :], "seq", 1)
        gate_pre, joined, filter_pre, mixed_part, packed, step_pre, steps, cum = with_scratch(
            functools.partial(scan_kernel, heads=heads),
            [
                ((rows, inner), f32),
                ((rows + EDGE, width), f32),
                ((rows, width), f32),
                ((rows, inner), f32),
                ((inner + EDGE, STATE), f32),
                ((rows, LANES), f32),
                ((rows, LANES), f32),
                ((rows, LANES), f32),
            ],
            "scan",
            [(rows, inner), (rows, inner)],
        )(
            normed, edge, w["gate"], w["value"], w["state"], w["step"], w["filt"], w["filt_bias"],
            w["bias"], w["rate"], w["skip"], marks, seg_row,
        )
        state_in = prefix(packed, 1, inner)
        mixed_pre, gated, squares = with_scratch(
            functools.partial(gate_kernel, heads=heads),
            [((rows, inner), f32), ((rows, inner), f32), ((8, rows), f32)],
            "gate",
            [(rows, inner)],
        )(mixed_part, filter_pre, gate_pre, cum, state_in, marks)
        unit, branch, scale_row = call(
            out_kernel, [((rows, inner), bf16), ((rows, D), f32), ((8, rows), f32)], "out"
        )(gated, w["gain"], w["out"], *copies_over(squares, "head"))
        kept.append(
            dict(
                normed=normed, gate_pre=gate_pre, joined=joined, filter_pre=filter_pre, packed=packed,
                step_pre=step_pre, steps=steps, cum=cum, state_in=state_in, mixed_pre=mixed_pre, gated=gated,
                scale_row=scale_row, unit=unit, stream_rows=stream_rows, stream_columns=stream_columns,
                scale_rows=scale_rows, scale_full=scale_full,
            )
        )
        if l < LAYERS - 1:
            stream_rows = stream_rows + scatter_sum(branch.reshape(head_count, part_rows, D), "head")
            scale_rows = lax.rsqrt(jnp.mean(stream_rows * stream_rows, axis=1) + epsilon)
            normed_rows = (stream_rows * scale_rows[:, None] * norm_gain[l + 1][None, :]).astype(bf16)
            normed = lax.all_gather(normed_rows, "head", axis=0, tiled=True)
            stream_columns = to_columns(stream_rows)
            scale_full = None
        else:
            blocks = branch.reshape(rows, head_count, share).transpose(1, 0, 2)
            mixed = (stream_columns + scatter_sum(blocks, "head")).astype(bf16)

    def pieces_sum(matrix):
        blocks = matrix.reshape(seq_count, D // seq_count, matrix.shape[1])
        got = lax.all_to_all(blocks, "seq", 0, 0, tiled=True)
        return jnp.sum(got.astype(f32), axis=0)

    norm_grads = [None] * LAYERS
    early = [None] * LAYERS
    late = [None] * LAYERS
    small = [None] * LAYERS
    state_rows = [None] * LAYERS
    residual_rows = None
    residual_columns = columns(cotangent)
    grad_rows = cotangent.astype(bf16)
    for l in reversed(range(LAYERS)):
        w = weights[l]
        k = kept[l]
        unit_grad, inner_sum = call(unit_kernel, [((rows, inner), f32), ((8, rows), f32)], "unit_grad")(
            grad_rows, w["out"], w["gain"], k["gated"]
        )
        mixed_grad, gate_low, grad_packed, gain_rows = with_scratch(
            functools.partial(gated_kernel, heads=heads),
            [((rows, inner), f32), ((rows, inner), bf16), ((inner + EDGE, STATE), f32), ((8, inner), f32)],
            "gated_grad",
            [(rows, inner)],
        )(
            unit_grad, k["gated"], k["gate_pre"], k["mixed_pre"], w["gain"], k["scale_row"], k["filter_pre"],
            k["cum"], marks, *copies_over(inner_sum, "head"),
        )
        later = prefix(grad_packed, -1, inner)
        grad_out = dot_first(grad_rows, k["unit"]).astype(bf16)
        grad_gate = dot_first(k["normed"], gate_low).astype(bf16)
        early[l] = pieces_sum(jnp.concatenate([grad_out, grad_gate], axis=1))
        stepped_grad, b_grad, c_grad, out_dot = with_scratch(
            functools.partial(scan_grad_kernel, heads=heads),
            [((rows, inner), f32), ((rows, STATE), f32), ((rows, STATE), f32), ((rows, LANES), f32)],
            "scan_grad",
            [(rows, inner), (rows, inner)],
        )(
            mixed_grad, k["filter_pre"], k["mixed_pre"], k["cum"], k["steps"], k["state_in"], w["skip"], marks,
            seg_row,
        )
        joined_grad, step_low, filter_rows = with_scratch(
            functools.partial(filter_grad_kernel, heads=heads),
            [((rows + EDGE, width), f32), ((rows, LANES), bf16), ((8, width), f32)],
            "filter_grad",
            [(rows, inner), (rows, inner), (rows + 2 * EDGE, width), (inner, STATE)],
        )(
            later, k["packed"], k["state_in"], stepped_grad, b_grad, c_grad, out_dot, mixed_grad, k["filter_pre"],
            k["joined"], k["cum"], k["steps"], k["step_pre"], w["rate"], w["skip"], marks, marks_ahead, w["filt"],
        )
        edge_grad = shifted(joined_grad[:EDGE], "seq", -1)
        normed_part, dots, value_low, state_grad = with_scratch(
            normed_grad_kernel,
            [((rows, D), f32), ((8, rows), f32), ((rows, inner), bf16), ((rows, 2 * STATE), f32)],
            "normed_grad",
            [(rows, width)],
        )(
            joined_grad, edge_grad, gate_low, step_low, k["normed"], w["gate"], w["value"], w["state"], w["step"]
        )
        if l > 0:
            total = scatter_sum(normed_part.reshape(head_count, part_rows, D), "head")
            normed_rows = own_rows(k["normed"]).astype(f32)
            mean_dot = jnp.mean(normed_rows * total, axis=1)
            norm_rows = k["stream_rows"] * k["scale_rows"][:, None]
            residual_rows = own_rows(cotangent) if residual_rows is None else residual_rows
            residual_rows = residual_rows + k["scale_rows"][:, None] * (
                norm_gain[l][None, :] * total - norm_rows * mean_dot[:, None]
            )
            grad_rows = lax.all_gather(residual_rows.astype(bf16), "head", axis=0, tiled=True)
            residual_columns = to_columns(residual_rows)
            norm_grads[l] = jnp.sum(total * norm_rows, axis=0)
        else:
            blocks = normed_part.reshape(rows, head_count, share).transpose(1, 0, 2)
            total = scatter_sum(blocks, "head")
            dot_total = functools.reduce(jnp.add, copies_over(dots, "head"))
            mean_dot = dot_total[0] / D
            norm_columns = k["stream_columns"] * k["scale_full"][:, None]
            residual_columns = residual_columns + k["scale_full"][:, None] * (
                columns(norm_gain[l])[None, :] * total - norm_columns * mean_dot[:, None]
            )
            norm_grads[l] = jnp.sum(total * norm_columns, axis=0)
        blocks = state_grad.reshape(rows, head_count, state_share).transpose(1, 0, 2)
        state_rows[l] = scatter_sum(blocks, "head")
        grad_value = dot_first(k["normed"], value_low).astype(bf16)
        grad_step = dot_first(k["normed"], step_low).astype(bf16)[:, :state_share]
        grad_state = dot_first(k["normed"].astype(f32), state_rows[l], highest).astype(bf16)
        late[l] = (pieces_sum(grad_value), pieces_sum(jnp.concatenate([grad_state, grad_step], axis=1)))
        small[l] = (gain_rows, filter_rows)

    def head_part(l):
        total = functools.reduce(jnp.add, copies_over(small[l][1][:, : 2 * STATE], "head"))
        return lax.dynamic_slice_in_dim(total, me * state_share, state_share, 1)

    def full_norm(l):
        if l == 0:
            return norm_grads[0]
        total = functools.reduce(jnp.add, copies_over(norm_grads[l].reshape(D // LANES, LANES), "head"))
        return columns(total.reshape(D))

    local = []
    for l in range(LAYERS):
        gain_rows, filter_rows = small[l]
        skip_grad = jnp.sum(gain_rows[1].reshape(heads, HEADDIM), axis=1)
        shared = head_part(l)
        local.append(
            [
                full_norm(l),
                filter_rows[5, :heads],
                filter_rows[6, :heads],
                skip_grad,
                filter_rows[:CONV, 2 * STATE :].reshape(-1),
                filter_rows[CONV, 2 * STATE :],
                shared[:CONV].reshape(-1),
                shared[CONV],
                gain_rows[0],
            ]
        )
    flat = jnp.concatenate([piece for one in local for piece in one])
    size = flat.shape[0]
    padded = -(-size // (8 * LANES)) * 8 * LANES
    summed = butterfly_sum(jnp.pad(flat, (0, padded - size)).reshape(-1, LANES), "seq").reshape(-1)
    found = []
    at = 0
    for one in local:
        row = []
        for piece in one:
            row.append(summed[at : at + piece.shape[0]])
            at += piece.shape[0]
        found.append(row)

    def stacked(which, shape=None):
        parts = [found[l][which] for l in range(LAYERS)]
        if shape is not None:
            parts = [part.reshape(shape) for part in parts]
        return jnp.stack(parts, axis=0)

    def both(pick):
        return jnp.stack([pick(l) for l in range(LAYERS)], axis=0)

    return (
        mixed,
        residual_columns,
        stacked(0),
        both(lambda l: early[l][:, inner:]),
        both(lambda l: late[l][0]),
        both(lambda l: late[l][1][:, :state_share]),
        both(lambda l: late[l][1][:, state_share : state_share + heads]),
        stacked(1),
        stacked(2),
        stacked(3),
        stacked(4, (CONV, inner)),
        stacked(5),
        stacked(6, (CONV, state_share)),
        stacked(7),
        stacked(8),
        both(lambda l: early[l][:, :inner].T),
    )


def solution(mesh):
    placed = (
        P("seq", None),
        P("seq", None),
        P(),
        P(),
        P(None, None, "head"),
        P(None, None, "head"),
        P(),
        P(None, None, "head"),
        P(None, "head"),
        P(None, "head"),
        P(None, "head"),
        P(None, None, "head"),
        P(None, "head"),
        P(),
        P(),
        P(None, "head"),
        P(None, "head", None),
    )
    return jax.shard_map(
        body,
        mesh=mesh,
        in_specs=placed,
        out_specs=(
            P("seq", "head"),
            P("seq", "head"),
            P(None, "head"),
            P(None, "seq", "head"),
            P(None, "seq", "head"),
            P(None, "seq", "head"),
            P(None, "seq", "head"),
            P(None, "head"),
            P(None, "head"),
            P(None, "head"),
            P(None, None, "head"),
            P(None, "head"),
            P(None, None, "head"),
            P(None, "head"),
            P(None, "head"),
            P(None, "head", "seq"),
        ),
        check_vma=False,
    )
```

```python
import functools
from types import SimpleNamespace

import jax
import jax.numpy as jnp
from jax import lax
from jax.experimental import pallas as pl
from jax.experimental.pallas import tpu as pltpu
from jax.sharding import PartitionSpec as P


D = 768
HEADDIM = 64
STATE = 128
CONV = 4
LAYERS = 2
INNER = 1536
LANES = 128
EDGE = 8
FAN = 4

epsilon = 1e-05
highest = lax.Precision.HIGHEST
high = lax.Precision.HIGH
f32 = jnp.float32
bf16 = jnp.bfloat16


def shifted(value, axis, by):
    count = lax.axis_size(axis)
    pairs = [(i, i + by) for i in range(count) if 0 <= i + by < count]
    return lax.ppermute(value, axis, pairs)


def partner(value, axis, mask):
    count = lax.axis_size(axis)
    return lax.ppermute(value, axis, [(i, i ^ mask) for i in range(count)])


def copies_over(value, axis):
    return [value] + [partner(value, axis, k) for k in range(1, lax.axis_size(axis))]


def butterfly_sum(value, axis):
    mask = 1
    while mask < lax.axis_size(axis):
        got = partner(value, axis, mask)
        value = value + got
        mask *= 2
    return value


def scatter_relative(keep, give, axis):
    got = partner(give, axis, 1)
    mask = 2
    while keep.shape[0] > 1:
        away = keep[1::2] + got[1::2]
        keep = keep[0::2] + got[0::2]
        got = partner(away, axis, mask)
        mask *= 2
    return keep[0], got[0]


SMEM = "smem"


def run(kernel, ins, outs, scratch=(), flops=1 << 28):
    specs, arrays = [], []
    for item in ins:
        if isinstance(item, tuple) and item[1] is SMEM:
            arrays.append(item[0])
            specs.append(pl.BlockSpec(memory_space=pltpu.SMEM))
        elif isinstance(item, tuple):
            array, layer = item
            arrays.append(array)
            rest = array.ndim - 1
            specs.append(
                pl.BlockSpec((None,) + array.shape[1:], functools.partial(lambda at, n, _: (at,) + (0,) * n, layer, rest))
            )
        else:
            arrays.append(item)
            specs.append(pl.BlockSpec(memory_space=pltpu.VMEM))
    return pl.pallas_call(
        kernel,
        grid=(1,),
        in_specs=specs,
        out_specs=[pl.BlockSpec(memory_space=pltpu.VMEM)] * len(outs),
        out_shape=[jax.ShapeDtypeStruct(s, d) for s, d in outs],
        scratch_shapes=[pltpu.VMEM(s, d) for s, d in scratch],
        cost_estimate=pl.CostEstimate(flops=flops, transcendentals=1 << 19, bytes_accessed=4 << 20),
        compiler_params=pltpu.CompilerParams(vmem_limit_bytes=56 * 1024 * 1024),
    )(*arrays)


def dot(a, b, precision=None):
    return lax.dot_general(a, b, (((1,), (0,)), ((), ())), precision=precision, preferred_element_type=f32)


def dot_last(a, b, precision=None):
    return lax.dot_general(a, b, (((1,), (1,)), ((), ())), precision=precision, preferred_element_type=f32)


def dot_first(a, b, precision=None):
    return lax.dot_general(a, b, (((0,), (0,)), ((), ())), precision=precision, preferred_element_type=f32)


def row_sums(x):
    return dot_last(jnp.ones((8, x.shape[1]), f32), x, highest)


def head_picker(rows):
    i = lax.broadcasted_iota(jnp.int32, (rows, LANES), 0)
    lane = lax.broadcasted_iota(jnp.int32, (rows, LANES), 1)
    return ((i >= lane * HEADDIM) & (i < (lane + 1) * HEADDIM)).astype(f32)


def spread(ref, columns, rows, heads):
    for k in range(heads):
        ref[:, k * HEADDIM : (k + 1) * HEADDIM] = jnp.broadcast_to(columns[:, k : k + 1], (rows, HEADDIM))
    return ref[...]


def silu(x):
    return x * jax.nn.sigmoid(x)


def silu_and_grad(x):
    s = jax.nn.sigmoid(x)
    return x * s, s * (1.0 + x * (1.0 - s))


def document(place, position):
    start = jnp.int32(0)
    found = jnp.zeros(jnp.shape(position), jnp.int32) - 1
    for k in range(place.shape[0] - 3):
        found = found + jnp.where(position >= start, 1, 0)
        start = start + place[3 + k]
    return found


def column_documents(place, rows, offset):
    at = lax.broadcasted_iota(jnp.int32, (rows, 1), 0)
    return document(place, at + (place[0] + offset))


def marks_kernel(place, marks, ahead, seg_row):
    rows = marks.shape[0]
    own = column_documents(place, rows, 0)
    before = document(place, place[0] - 1)
    end = document(place, place[0] + rows - 1)
    lane = lax.broadcasted_iota(jnp.int32, (rows, LANES), 1)
    found = jnp.zeros((rows, LANES), f32)
    columns = [(own == column_documents(place, rows, -k)).astype(f32) for k in range(CONV)]
    columns += [(own == before).astype(f32), (own == end).astype(f32), own.astype(f32)]
    columns += [jnp.where(end == before, 1.0, 0.0).astype(f32)]
    for k, column in enumerate(columns):
        found = jnp.where(lane == k, column, found)
    marks[...] = found
    reader = column_documents(place, rows + EDGE, -EDGE)
    lane = lax.broadcasted_iota(jnp.int32, (rows + EDGE, LANES), 1)
    found = jnp.zeros((rows + EDGE, LANES), f32)
    for k in range(CONV):
        found = jnp.where(lane == k, (column_documents(place, rows + EDGE, k - EDGE) == reader).astype(f32), found)
    ahead[...] = found
    seg_row[...] = document(place, lax.broadcasted_iota(jnp.int32, (8, rows), 1) + place[0]).astype(f32)


def pair_bias(marks, seg_row):
    rows = marks.shape[0]
    i = lax.broadcasted_iota(jnp.int32, (rows, rows), 0)
    j = lax.broadcasted_iota(jnp.int32, (rows, rows), 1)
    return jnp.where((i >= j) & (marks[:, 6:7] == seg_row[0:1, :]), 0.0, -1e30)


def pack(packed, state, decay):
    packed[: state.shape[0], :] = state
    packed[state.shape[0] :, :] = jnp.broadcast_to(decay, (EDGE, LANES))


def add_far(far, old, state_out):
    count = state_out.shape[0]
    if not far:
        state_out[...] = old[0][...]
        return
    for k in range(count // HEADDIM):
        at = slice(k * HEADDIM, (k + 1) * HEADDIM)
        state = far[0][at, :]
        if old:
            state = old[0][at, :] + jnp.broadcast_to(old[1][0:1, k : k + 1], (HEADDIM, STATE)) * state
        state_out[at, :] = state


def lane_row(ref, l, heads, scr):
    scr[...] = jnp.zeros(scr.shape, f32)
    scr[0:1, :heads] = ref[l : l + 1, :]
    return scr[0:1, :]


def state_kernel(marks_ref, x_ref, edge_ref, *refs, layer, heads, norm):
    if norm:
        gain, refs = refs[0], refs[1:]
    (value_w, state_w, step_w, filt_state, filt_value, state_bias, value_bias, step_bias, decay_log) = refs[:9]
    refs = refs[9:]
    if norm:
        normed_out, scale_out = refs[:2]
        refs = refs[2:]
    joined, filter_pre, active, step_pre, steps_out, cum_out, state_out, packed, tail_scr, lane_scr, row_scr = refs
    rows = x_ref.shape[0]
    marks = marks_ref[...]
    if norm:

        def normalise(raw):
            raw = raw.astype(f32)
            scale = lax.rsqrt(jnp.mean(raw * raw, axis=1, keepdims=True) + epsilon)
            return (raw * scale * gain[layer : layer + 1, :]).astype(bf16), scale

        x, scale = normalise(x_ref[...])
        e, _ = normalise(edge_ref[...])
        normed_out[...] = x
        scale_out[...] = jnp.broadcast_to(scale, scale_out.shape)
    else:
        x = x_ref[...]
        e = edge_ref[...]
    joined[EDGE:, : 2 * STATE] = dot(x, state_w[...])
    joined[EDGE:, 2 * STATE :] = dot(x, value_w[...])
    joined[:EDGE, : 2 * STATE] = dot(e, state_w[...])[EDGE:]
    joined[:EDGE, 2 * STATE :] = dot(e, value_w[...])[EDGE:]
    lane_scr[...] = jnp.zeros(lane_scr.shape, f32)
    lane_scr[:, :heads] = dot_last(x, step_w[...]) + step_bias[layer : layer + 1, :]
    for at, taps_w, bias in (
        (slice(0, 2 * STATE), filt_state, state_bias),
        (slice(2 * STATE, joined.shape[1]), filt_value, value_bias),
    ):
        pre = bias[layer : layer + 1, :] + taps_w[0:1, :] * joined[EDGE:, at]
        for k in range(1, CONV):
            pre = pre + taps_w[k : k + 1, :] * joined[EDGE - k : EDGE - k + rows, at] * marks[:, k : k + 1]
        filter_pre[:, at] = pre
        active[:, at] = silu(pre)
    b = active[:, :STATE]
    values = active[:, 2 * STATE :]
    pre_step = lane_scr[...]
    steps = jnp.maximum(pre_step, 0.0) + jnp.log1p(jnp.exp(-jnp.abs(pre_step)))
    i = lax.broadcasted_iota(jnp.int32, (rows, rows), 0)
    j = lax.broadcasted_iota(jnp.int32, (rows, rows), 1)
    rate = lane_row(decay_log, layer, heads, row_scr)
    cum = dot((i >= j).astype(f32), steps * -jnp.exp(rate), highest)
    step_pre[...] = pre_step
    steps_out[...] = steps
    cum_out[...] = cum
    last = cum[rows - 1 : rows, :]
    tail = jnp.exp(last - cum) * marks[:, 5:6] * steps
    state = dot_first(spread(tail_scr, tail, rows, heads) * values, b, high)
    state_out[...] = state
    pack(packed, state, jnp.exp(last) * marks[0:1, 7:8])


def local_kernel(
    marks, seg_row, normed, gate_w, active, steps, cum, skip, gate_pre, mixed_part, step_scr, *, layer, heads
):
    rows = normed.shape[0]
    half = rows // 2
    gate_pre[...] = dot(normed[...], gate_w[...])
    cum = cum[...]
    cum_t = cum.T
    step_scr[...] = spread(step_scr, steps[...], rows, heads) * active[:, 2 * STATE :]
    bias = pair_bias(marks[...], seg_row[...])
    for low, top in ((0, half), (half, rows)):
        here = bias[low:top, :top]
        scores = dot_last(active[low:top, STATE : 2 * STATE], active[:top, :STATE], high)
        for k in range(heads):
            at = slice(k * HEADDIM, (k + 1) * HEADDIM)
            source = slice(2 * STATE + k * HEADDIM, 2 * STATE + (k + 1) * HEADDIM)
            weights = scores * jnp.exp(cum[low:top, k : k + 1] - cum_t[k : k + 1, :top] + here)
            mixed_part[low:top, at] = (
                dot(weights, step_scr[:top, at], high) + skip[layer : layer + 1, k : k + 1] * active[low:top, source]
            )


def combine_kernel(place, *refs, span, sign, first):
    parts, refs = refs[:FAN], refs[FAN:]
    if not first:
        old, refs = refs[:2], refs[2:]
    state_out, decay_out, packed = refs
    count = state_out.shape[0]
    mine = lax.rem(lax.div(place[2], jnp.int32(span)), jnp.int32(FAN))

    def flag(condition):
        return jnp.where(condition, 1.0, 0.0).astype(f32)

    rows = [part[count : count + 1, :] for part in parts]
    chosen = [[flag((mine ^ r) == j) for j in range(FAN)] for r in range(FAN)]
    decay = [sum(chosen[r][j] * rows[r] for r in range(FAN)) for j in range(FAN)]
    order = range(FAN) if sign > 0 else range(FAN - 1, -1, -1)
    through = jnp.ones((1, LANES), f32)
    total = jnp.ones((1, LANES), f32)
    here = [None] * FAN
    whole = [None] * FAN
    for j in reversed(order):
        between = flag((mine - j) * sign > 0)
        here[j] = between * through
        whole[j] = total
        through = through * (between * decay[j] + (1.0 - between))
        total = total * decay[j]
    weight_here = [sum(chosen[r][j] * here[j] for j in range(FAN)) for r in range(FAN)]
    weight_whole = [sum(chosen[r][j] * whole[j] for j in range(FAN)) for r in range(FAN)]
    decay_out[...] = jnp.broadcast_to(through if first else old[1][0:1, :] * through, decay_out.shape)
    packed[count:, :] = jnp.broadcast_to(total, (EDGE, LANES))
    for k in range(count // HEADDIM):
        at = slice(k * HEADDIM, (k + 1) * HEADDIM)

        def wide(row):
            return jnp.broadcast_to(row[:, k : k + 1], (HEADDIM, STATE))

        values = [part[at, :] for part in parts]
        state = sum(wide(weight_here[r]) * values[r] for r in range(1, FAN))
        if not first:
            state = old[0][at, :] + wide(old[1][0:1, :]) * state
        state_out[at, :] = state
        packed[at, :] = sum(wide(weight_whole[r]) * values[r] for r in range(FAN))


def prefix(place, packed, sign, rows):
    count = lax.axis_size("seq")
    old = []
    span = 1
    while count // span > 2:
        parts = [packed] + [partner(packed, "seq", r * span) for r in range(1, FAN)]
        *old, packed = run(
            functools.partial(combine_kernel, span=span, sign=sign, first=not old),
            [place] + parts + old,
            [((rows, STATE), f32), ((EDGE, LANES), f32), ((rows + EDGE, STATE), f32)],
        )
        span *= FAN
    if count == span:
        return [], old
    return [shifted(packed, "seq", sign * span)], old


def gate_kernel(marks, mixed_part, active, gate_pre, cum, *refs, heads, fars):
    far, old = refs[:fars], refs[fars:-5]
    state_in, mixed_pre, gated, squares, scr = refs[-5:]
    rows = mixed_part.shape[0]
    add_far(far, old, state_in)
    carried = dot_last(active[:, STATE : 2 * STATE], state_in[...], high)
    entering = spread(scr, jnp.exp(cum[...]) * marks[:, 4:5], rows, heads)
    mixed = mixed_part[...] + entering * carried
    mixed_pre[...] = mixed
    out = mixed * silu(gate_pre[...])
    gated[...] = out
    squares[...] = row_sums(out * out)


def relative_blocks(place, scr, keep, give):
    size = keep.shape[1]
    for r in range(keep.shape[0]):
        keep[r] = scr[pl.ds(pl.multiple_of((place[1] ^ (2 * r)) * size, 8), size), :]
        give[r] = scr[pl.ds(pl.multiple_of((place[1] ^ (2 * r + 1)) * size, 8), size), :]


def out_kernel(place, gated, gain, out_w, *refs, layer):
    parts, (unit, scale_row, keep, give, scr) = refs[:-5], refs[-5:]
    total = parts[0][...]
    for part in parts[1:]:
        total = total + part[...]
    scale = lax.rsqrt(total / INNER + epsilon)
    scale_row[...] = scale
    column = scale.T[:, 0:1]
    rows = (gated[...] * column * gain[layer : layer + 1, :]).astype(bf16)
    unit[...] = rows
    scr[...] = dot(rows, out_w[...])
    relative_blocks(place, scr, keep, give)


def unit_kernel(grad_rows, out_w, gain, gated, unit_grad, inner, *, layer):
    grad = dot_last(grad_rows[...], out_w[...])
    unit_grad[...] = grad
    inner[...] = row_sums(gain[layer : layer + 1, :] * grad * gated[...])


def gated_kernel(
    marks, unit_grad, gated, gate_pre, mixed_pre, gain, scale_row, active, cum, *refs, heads, layer
):
    parts = refs[:-5]
    mixed_grad, gate_low, packed, row_out, scr = refs[-5:]
    rows = gated.shape[0]
    total = parts[0][...]
    for part in parts[1:]:
        total = total + part[...]
    scale = scale_row[...]
    cube = (scale * scale * scale * total / INNER).T[:, 0:1]
    column = scale.T[:, 0:1]
    grad = unit_grad[...]
    kept = gated[...]
    gated_grad = column * (gain[layer : layer + 1, :] * grad) - kept * cube
    level, slope = silu_and_grad(gate_pre[...])
    mixed = gated_grad * level
    mixed_grad[...] = mixed
    gate_low[...] = (gated_grad * mixed_pre[...] * slope).astype(bf16)
    row_out[...] = jnp.zeros(row_out.shape, f32)
    row_out[5:6, :] = jnp.sum(grad * kept * column, axis=0, keepdims=True)
    row_out[6:7, :] = jnp.sum(mixed * active[:, 2 * STATE :], axis=0, keepdims=True)
    cum = cum[...]
    entering = spread(scr, jnp.exp(cum) * marks[:, 4:5], rows, heads)
    state = dot_first(mixed * entering, active[:, STATE : 2 * STATE], high)
    pack(packed, state, jnp.exp(cum[rows - 1 : rows, :]) * marks[0:1, 7:8])


def scan_grad_kernel(
    marks_ref, seg_row, mixed_grad, active, mixed_pre, cum, steps, state_in, skip, grad_rows, unit, normed, gate_low,
    stepped_grad, b_grad, c_grad, out_dot, early, full_scr, step_scr, score_scr, *, heads, layer,
):
    rows = mixed_grad.shape[0]
    half = rows // 2
    inner = heads * HEADDIM
    marks = marks_ref[...]
    early[:, :inner] = dot_first(grad_rows[...], unit[...]).astype(bf16)
    early[:, inner:] = dot_first(normed[...], gate_low[...]).astype(bf16)
    values = active[:, 2 * STATE :]
    cum = cum[...]
    cum_t = cum.T
    grad = mixed_grad[...]
    entering = spread(full_scr, jnp.exp(cum) * marks[:, 4:5], rows, heads)
    direct = dot(grad * entering, state_in[...], high)
    for k in range(heads):
        at = slice(k * HEADDIM, (k + 1) * HEADDIM)
        step_scr[0:1, at] = jnp.broadcast_to(skip[layer : layer + 1, k : k + 1], (1, HEADDIM))
    out_dot[...] = dot(grad * (mixed_pre[...] - step_scr[0:1, :] * values), head_picker(inner), highest)
    step_scr[...] = spread(step_scr, steps[...], rows, heads) * values
    bias = pair_bias(marks, seg_row[...])
    score_scr[:half, half:] = jnp.zeros((half, rows - half), f32)
    for low, top in ((0, half), (half, rows)):
        here = bias[low:top, :top]
        scores = dot_last(active[low:top, STATE : 2 * STATE], active[:top, :STATE], high)
        score_grad = jnp.zeros((top - low, top), f32)
        for k in range(heads):
            at = slice(k * HEADDIM, (k + 1) * HEADDIM)
            decays = jnp.exp(cum[low:top, k : k + 1] - cum_t[k : k + 1, :top] + here)
            own = mixed_grad[low:top, at]
            score_grad = score_grad + decays * dot_last(own, step_scr[:top, at], high)
            found = dot_first(own, scores * decays, high).T
            if low == 0:
                stepped_grad[:top, at] = found
                stepped_grad[top:, at] = jnp.zeros((rows - top, HEADDIM), f32)
            else:
                stepped_grad[:, at] = stepped_grad[:, at] + found
        score_scr[low:top, :top] = score_grad
    total = score_scr[...]
    c_grad[...] = dot(total, active[:, :STATE], high) + direct
    b_grad[...] = dot_first(total, active[:, STATE : 2 * STATE], high)


def filter_grad_kernel(
    marks_ref, ahead, local_state, state_in, stepped_grad, b_grad, c_grad, out_dot, mixed_grad, filter_pre, active, joined, cum,
    steps, step_pre, decay_log, skip, filt_state, filt_value, row_in, *refs, heads, layer, fars,
):
    far, old = refs[:fars], refs[fars:-12]
    joined_grad, edge_out, step_low, row_out, shared_out = refs[-12:-7]
    tail_scr, step_scr, skip_scr, pad_scr, state_scr, later, lane_scr = refs[-7:]
    add_far(far, old, later)
    rows = mixed_grad.shape[0]
    inner = heads * HEADDIM
    marks = marks_ref[...]
    b = active[:, :STATE]
    values = active[:, 2 * STATE :]
    cum = cum[...]
    step = steps[...]
    last = cum[rows - 1 : rows, :]
    tail = jnp.exp(last - cum) * marks[:, 5:6]
    late = later[...]
    rate = -jnp.exp(lane_row(decay_log, layer, heads, lane_scr))
    tail_full = spread(tail_scr, tail, rows, heads)
    step_full = spread(step_scr, step, rows, heads)
    for k in range(heads):
        at = slice(k * HEADDIM, (k + 1) * HEADDIM)
        skip_scr[0:1, at] = jnp.broadcast_to(skip[layer : layer + 1, k : k + 1], (1, HEADDIM))
    total = stepped_grad[...] + tail_full * dot_last(b, late, high)
    value_grad = step_full * total + skip_scr[0:1, :] * mixed_grad[...]
    b_total = b_grad[...] + dot(tail_full * step_full * values, late, high)
    picker = head_picker(inner)
    step_direct = dot(total * values, picker, highest)
    through = jnp.exp(last) * marks[0:1, 7:8]
    for k in range(heads):
        at = slice(k * HEADDIM, (k + 1) * HEADDIM)
        state_scr[at, :] = late[at, :] * (
            local_state[at, :] + jnp.broadcast_to(through[:, k : k + 1], (HEADDIM, STATE)) * state_in[at, :]
        )
    end = dot(row_sums(state_scr[...]), picker, highest)[0:1, :]
    i = lax.broadcasted_iota(jnp.int32, (rows, rows), 0)
    j = lax.broadcasted_iota(jnp.int32, (rows, rows), 1)
    log_grad = dot((i <= j).astype(f32), out_dot[...] - step * step_direct, highest) + end
    step_grad = (step_direct + rate * log_grad) * jax.nn.sigmoid(step_pre[...])
    step_low[...] = step_grad.astype(bf16)
    width = pad_scr.shape[1]
    pad_scr[:EDGE, :] = jnp.zeros((EDGE, width), f32)
    pad_scr[EDGE + rows :, :] = jnp.zeros((EDGE, width), f32)
    for at, grad in (
        (slice(0, STATE), b_total),
        (slice(STATE, 2 * STATE), c_grad[...]),
        (slice(2 * STATE, width), value_grad),
    ):
        pad_scr[EDGE : EDGE + rows, at] = grad * silu_and_grad(filter_pre[:, at])[1]
    shared_out[...] = jnp.zeros(shared_out.shape, f32)
    row_out[...] = row_in[...]
    for at, taps_w, out in (
        (slice(0, 2 * STATE), filt_state, shared_out.at[:, : 2 * STATE]),
        (slice(2 * STATE, width), filt_value, row_out),
    ):
        grad = taps_w[0:1, :] * pad_scr[: EDGE + rows, at]
        for k in range(1, CONV):
            grad = grad + taps_w[k : k + 1, :] * pad_scr[k : k + EDGE + rows, at] * ahead[:, k : k + 1]
        joined_grad[:, at] = grad[EDGE:]
        edge_out[:, at] = grad[:EDGE]
        own = pad_scr[EDGE : EDGE + rows, at]
        for k in range(CONV):
            masked = own * joined[EDGE - k : EDGE - k + rows, at]
            if k > 0:
                masked = masked * marks[:, k : k + 1]
            out[k : k + 1, :] = jnp.sum(masked, axis=0, keepdims=True)
        out[4:5, :] = jnp.sum(own, axis=0, keepdims=True)
    row_out[7:8, :heads] = jnp.sum(step_grad, axis=0, keepdims=True)[:, :heads]
    row_out[7:8, HEADDIM : HEADDIM + heads] = (jnp.sum(step * log_grad, axis=0, keepdims=True) * rate)[:, :heads]


def normed_grad_kernel(
    place, joined_grad, edge_grad, gate_low, step_low, gate_w, value_w, state_w, step_w, shared_in, *refs, heads, last
):
    rows = joined_grad.shape[0]
    shared_out, keep, give, value_low, state_keep, state_give, scr, part_scr = refs[-8:]
    scr[...] = joined_grad[...]
    scr[rows - EDGE :, :] = scr[rows - EDGE :, :] + edge_grad[...]
    low = scr[:, 2 * STATE :].astype(bf16)
    value_low[...] = low
    size = state_keep.shape[2]
    for k in range(2 * STATE // size):
        relative = place[1] ^ k

        @pl.when((relative & 1) == 0)
        def _():
            state_keep[relative >> 1] = scr[:, k * size : (k + 1) * size]

        @pl.when((relative & 1) == 1)
        def _():
            state_give[relative >> 1] = scr[:, k * size : (k + 1) * size]

    part = (
        dot_last(gate_low[...], gate_w[...])
        + dot_last(low, value_w[...])
        + dot(step_low[:, :heads], step_w[...])
        + dot_last(scr[:, : 2 * STATE], state_w[...].astype(f32), high)
    )
    part_scr[...] = part
    relative_blocks(place, part_scr, keep, give)
    shared_out[...] = shared_in[...]
    if last:
        tokens, scale = refs[:2]
        norm_rows = tokens[...].astype(f32) * scale[:, 0:1]
        shared_out[5:6, :] = jnp.sum(part * norm_rows, axis=0, keepdims=True)


def late_kernel(normed, value_low, step_low, state_a, state_b, late):
    x = normed[...]
    inner = value_low.shape[1]
    size = state_a.shape[1]
    late[:, :inner] = dot_first(x, value_low[...]).astype(bf16)
    late[:, inner : inner + size] = dot_first(x.astype(f32), state_a[...] + state_b[...], high).astype(bf16)
    late[:, inner + size :] = dot_first(x, step_low[...]).astype(bf16)


def step(
    tokens,
    cotangent,
    doc_lengths,
    norm_gain,
    gate_proj,
    value_proj,
    state_proj,
    step_proj,
    step_bias,
    decay_log,
    skip_gain,
    filter_value,
    filter_value_bias,
    filter_state,
    filter_state_bias,
    gated_gain,
    out_proj,
):
    rows = tokens.shape[0]
    head_count = lax.axis_size("head")
    seq_count = lax.axis_size("seq")
    me = lax.axis_index("head")
    inner = gate_proj.shape[2]
    heads = step_proj.shape[2]
    width = 2 * STATE + inner
    share = D // head_count
    part_rows = rows // head_count
    state_share = 2 * STATE // head_count
    half = head_count // 2

    def own_rows(matrix):
        return lax.dynamic_slice_in_dim(matrix, me * part_rows, part_rows, 0)

    at_seq = lax.axis_index("seq")
    numbers = jnp.concatenate(
        [jnp.stack([at_seq * rows, me, at_seq]).astype(jnp.int32), doc_lengths.astype(jnp.int32)]
    )
    place = (numbers, SMEM)
    step_rows = jnp.swapaxes(step_proj, 1, 2)
    marks, marks_ahead, seg_row = run(
        marks_kernel, [place], [((rows, LANES), f32), ((rows + EDGE, LANES), f32), ((8, rows), f32)]
    )

    kept = []
    stream_rows = own_rows(tokens).astype(f32)
    normed = None
    normed_rows = None
    scale_rows = None
    for l in range(LAYERS):
        source = tokens if l == 0 else normed
        edge = shifted(source[rows - 2 * EDGE :], "seq", 1)
        norm_outs = [((rows, D), bf16), ((rows, LANES), f32)] if l == 0 else []
        found = run(
            functools.partial(state_kernel, layer=l, heads=heads, norm=l == 0),
            [marks, source, edge]
            + ([norm_gain] if l == 0 else [])
            + [
                (value_proj, l),
                (state_proj, l),
                (step_rows, l),
                (filter_state, l),
                (filter_value, l),
                filter_state_bias,
                filter_value_bias,
                step_bias,
                decay_log,
            ],
            norm_outs
            + [
                ((rows + EDGE, width), f32),
                ((rows, width), f32),
                ((rows, width), f32),
                ((rows, LANES), f32),
                ((rows, LANES), f32),
                ((rows, LANES), f32),
                ((inner, STATE), f32),
                ((inner + EDGE, STATE), f32),
            ],
            [((rows, inner), f32), ((rows, LANES), f32), ((8, LANES), f32)],
        )
        scale_full = None
        if l == 0:
            normed, scale_full = found[:2]
            found = found[2:]
            normed_rows = own_rows(normed)
            scale_rows = own_rows(scale_full)[:, 0]
        joined, filter_pre, active, step_pre, steps, cum, local_state, packed = found
        gate_pre, mixed_part = run(
            functools.partial(local_kernel, layer=l, heads=heads),
            [marks, seg_row, normed, (gate_proj, l), active, steps, cum, skip_gain],
            [((rows, inner), f32), ((rows, inner), f32)],
            [((rows, inner), f32)],
        )
        far, old = prefix(place, packed, 1, inner)
        state_in, mixed_pre, gated, squares = run(
            functools.partial(gate_kernel, heads=heads, fars=len(far)),
            [marks, mixed_part, active, gate_pre, cum, *far, *old],
            [((inner, STATE), f32), ((rows, inner), f32), ((rows, inner), f32), ((8, rows), f32)],
            [((rows, inner), f32)],
        )
        square_parts = copies_over(squares, "head")
        unit, scale_row, keep, give = run(
            functools.partial(out_kernel, layer=l),
            [place, gated, gated_gain, (out_proj, l), *square_parts],
            [
                ((rows, inner), bf16),
                ((8, rows), f32),
                ((half, part_rows, D), f32),
                ((half, part_rows, D), f32),
            ],
            [((rows, D), f32)],
        )
        kept.append(
            SimpleNamespace(
                normed=normed, gate_pre=gate_pre, joined=joined, filter_pre=filter_pre, active=active, local_state=local_state,
                step_pre=step_pre, steps=steps, cum=cum, state_in=state_in, mixed_pre=mixed_pre, gated=gated,
                scale_row=scale_row, unit=unit, stream_rows=stream_rows, normed_rows=normed_rows,
                scale_rows=scale_rows, scale_full=scale_full,
            )
        )
        stream_rows = stream_rows + sum(scatter_relative(keep, give, "head"))
        if l < LAYERS - 1:
            scale_rows = lax.rsqrt(jnp.mean(stream_rows * stream_rows, axis=1) + epsilon)
            normed_rows = (stream_rows * scale_rows[:, None] * norm_gain[l + 1][None, :]).astype(bf16)
            normed = lax.all_gather(normed_rows, "head", axis=0, tiled=True)

    def pieces_sum(matrix):
        blocks = matrix.reshape(seq_count, D // seq_count, matrix.shape[1])
        got = lax.all_to_all(blocks, "seq", 0, 0, tiled=True)
        return jnp.sum(got.astype(f32), axis=0)

    early = [None] * LAYERS
    late = [None] * LAYERS
    local_rows = [None] * LAYERS
    shared_rows = [None] * LAYERS
    residual_rows = own_rows(cotangent)
    grad_rows = cotangent.astype(bf16)
    for l in reversed(range(LAYERS)):
        k = kept[l]
        unit_grad, inner_sum = run(
            functools.partial(unit_kernel, layer=l),
            [grad_rows, (out_proj, l), gated_gain, k.gated],
            [((rows, inner), f32), ((8, rows), f32)],
        )
        inner_parts = copies_over(inner_sum, "head")
        mixed_grad, gate_low, grad_packed, gain_rows = run(
            functools.partial(gated_kernel, heads=heads, layer=l),
            [
                marks, unit_grad, k.gated, k.gate_pre, k.mixed_pre, gated_gain, k.scale_row,
                k.active, k.cum, *inner_parts,
            ],
            [
                ((rows, inner), f32),
                ((rows, inner), bf16),
                ((inner + EDGE, STATE), f32),
                ((8, inner), f32),
            ],
            [((rows, inner), f32)],
        )
        stepped_grad, b_grad, c_grad, out_dot, early_part = run(
            functools.partial(scan_grad_kernel, heads=heads, layer=l),
            [
                marks, seg_row, mixed_grad, k.active, k.mixed_pre, k.cum, k.steps, k.state_in, skip_gain,
                grad_rows, k.unit, k.normed, gate_low,
            ],
            [
                ((rows, inner), f32),
                ((rows, STATE), f32),
                ((rows, STATE), f32),
                ((rows, LANES), f32),
                ((D, 2 * inner), bf16),
            ],
            [((rows, inner), f32), ((rows, inner), f32), ((rows, rows), f32)],
        )
        early[l] = pieces_sum(early_part)
        far, old = prefix(place, grad_packed, -1, inner)
        joined_grad, edge_out, step_low, local_rows[l], shared = run(
            functools.partial(filter_grad_kernel, heads=heads, layer=l, fars=len(far)),
            [
                marks, marks_ahead, k.local_state, k.state_in, stepped_grad, b_grad, c_grad, out_dot,
                mixed_grad, k.filter_pre, k.active, k.joined, k.cum, k.steps, k.step_pre, decay_log, skip_gain,
                (filter_state, l), (filter_value, l), gain_rows, *far, *old,
            ],
            [
                ((rows, width), f32),
                ((EDGE, width), f32),
                ((rows, LANES), bf16),
                ((8, inner), f32),
                ((8, D), f32),
            ],
            [
                ((rows, inner), f32),
                ((rows, inner), f32),
                ((8, inner), f32),
                ((rows + 2 * EDGE, width), f32),
                ((inner, STATE), f32),
                ((inner, STATE), f32),
                ((8, LANES), f32),
            ],
        )
        edge_grad = shifted(edge_out, "seq", -1)
        last = l == 0
        shared_rows[l], keep, give, value_low, state_keep, state_give = run(
            functools.partial(normed_grad_kernel, heads=heads, last=last),
            [
                place, joined_grad, edge_grad, gate_low, step_low, (gate_proj, l), (value_proj, l), (state_proj, l),
                (step_rows, l), shared,
            ]
            + ([tokens, k.scale_full] if last else []),
            [
                ((8, D), f32),
                ((half, part_rows, D), f32),
                ((half, part_rows, D), f32),
                ((rows, inner), bf16),
                ((half, rows, state_share), f32),
                ((half, rows, state_share), f32),
            ],
            [((rows, width), f32), ((rows, D), f32)],
        )
        total = sum(scatter_relative(keep, give, "head"))
        state_parts = scatter_relative(state_keep, state_give, "head")
        mean_dot = jnp.mean(k.normed_rows.astype(f32) * total, axis=1)
        norm_rows = k.stream_rows * k.scale_rows[:, None]
        residual_rows = residual_rows + k.scale_rows[:, None] * (
            norm_gain[l][None, :] * total - norm_rows * mean_dot[:, None]
        )
        if not last:
            grad_rows = lax.all_gather(residual_rows.astype(bf16), "head", axis=0, tiled=True)
            fifth = (jnp.arange(8) == 5).astype(f32)
            shared_rows[l] = shared_rows[l] + fifth[:, None] * jnp.sum(total * norm_rows, axis=0)[None, :]
        (late_part,) = run(
            late_kernel, [k.normed, value_low, step_low, *state_parts], [((D, inner + state_share + LANES), bf16)]
        )
        late[l] = pieces_sum(late_part)

    pairs = jnp.concatenate(
        [
            stream_rows.reshape(part_rows, head_count, share),
            residual_rows.reshape(part_rows, head_count, share),
        ],
        axis=2,
    )
    got = [lax.dynamic_index_in_dim(pairs, me ^ r, 1, keepdims=False) for r in range(head_count)]
    got = [got[0]] + [partner(got[r], "head", r) for r in range(1, head_count)]
    placed = jnp.zeros((head_count, part_rows, 2 * share), f32)
    for r in range(head_count):
        placed = lax.dynamic_update_index_in_dim(placed, got[r], me ^ r, 0)
    placed = placed.reshape(rows, 2 * share)
    mixed = placed[:, :share].astype(bf16)
    residual_columns = placed[:, share:]

    shared = functools.reduce(jnp.add, copies_over(jnp.concatenate(shared_rows, axis=0), "head"))
    small = butterfly_sum(jnp.concatenate([shared, jnp.concatenate(local_rows, axis=0)], axis=1), "seq")
    shared = small[:, :D].reshape(LAYERS, 8, D)
    own = small[:, D:].reshape(LAYERS, 8, inner)
    filter_share = lax.dynamic_slice_in_dim(shared, me * state_share, state_share, 2)

    def both(pick):
        return jnp.stack([pick(l) for l in range(LAYERS)], axis=0)

    return (
        mixed,
        residual_columns,
        lax.dynamic_slice_in_dim(shared[:, 5], me * share, share, 1),
        both(lambda l: early[l][:, inner:]),
        both(lambda l: late[l][:, :inner]),
        both(lambda l: late[l][:, inner : inner + state_share]),
        both(lambda l: late[l][:, inner + state_share : inner + state_share + heads]),
        own[:, 7, :heads],
        own[:, 7, HEADDIM : HEADDIM + heads],
        jnp.sum(own[:, 6].reshape(LAYERS, heads, HEADDIM), axis=2),
        own[:, :CONV],
        own[:, CONV],
        filter_share[:, :CONV],
        filter_share[:, CONV],
        own[:, 5],
        both(lambda l: early[l][:, :inner].T),
    )


def solution(mesh):
    placed = (
        P("seq", None),
        P("seq", None),
        P(),
        P(),
        P(None, None, "head"),
        P(None, None, "head"),
        P(),
        P(None, None, "head"),
        P(None, "head"),
        P(None, "head"),
        P(None, "head"),
        P(None, None, "head"),
        P(None, "head"),
        P(),
        P(),
        P(None, "head"),
        P(None, "head", None),
    )
    return jax.shard_map(
        step,
        mesh=mesh,
        in_specs=placed,
        out_specs=(
            P("seq", "head"),
            P("seq", "head"),
            P(None, "head"),
            P(None, "seq", "head"),
            P(None, "seq", "head"),
            P(None, "seq", "head"),
            P(None, "seq", "head"),
            P(None, "head"),
            P(None, "head"),
            P(None, "head"),
            P(None, None, "head"),
            P(None, "head"),
            P(None, None, "head"),
            P(None, "head"),
            P(None, "head"),
            P(None, "head", "seq"),
        ),
        check_vma=False,
    )
```

```python
import functools
from types import SimpleNamespace

import jax
import jax.numpy as jnp
from jax import lax
from jax.experimental import pallas as pl
from jax.experimental.pallas import tpu as pltpu
from jax.sharding import PartitionSpec as P


D = 768
HEADDIM = 64
STATE = 128
CONV = 4
LAYERS = 2
INNER = 1536
LANES = 128
EDGE = 8
FAN = 4
PIECE = 256

epsilon = 1e-05
high = lax.Precision.HIGH
f32 = jnp.float32
bf16 = jnp.bfloat16


def shifted(value, axis, by):
    count = lax.axis_size(axis)
    pairs = [(i, i + by) for i in range(count) if 0 <= i + by < count]
    return lax.ppermute(value, axis, pairs)


def partner(value, axis, mask):
    count = lax.axis_size(axis)
    return lax.ppermute(value, axis, [(i, i ^ mask) for i in range(count)])


def copies_over(value, axis):
    return [value] + [partner(value, axis, k) for k in range(1, lax.axis_size(axis))]


def butterfly_sum(value, axis):
    mask = 1
    while mask < lax.axis_size(axis):
        got = partner(value, axis, mask)
        value = value + got
        mask *= 2
    return value


def scatter_relative(keep, give, axis):
    got = partner(give, axis, 1)
    mask = 2
    while keep.shape[0] > 1:
        away = keep[1::2] + got[1::2]
        keep = keep[0::2] + got[0::2]
        got = partner(away, axis, mask)
        mask *= 2
    return keep[0], got[0]


SMEM = "smem"


def run(kernel, ins, outs, scratch=(), flops=1 << 28):
    specs, arrays = [], []
    for item in ins:
        if isinstance(item, tuple) and item[1] is SMEM:
            arrays.append(item[0])
            specs.append(pl.BlockSpec(memory_space=pltpu.SMEM))
        elif isinstance(item, tuple):
            array, layer = item
            arrays.append(array)
            rest = array.ndim - 1
            specs.append(
                pl.BlockSpec((None,) + array.shape[1:], functools.partial(lambda at, n, _: (at,) + (0,) * n, layer, rest))
            )
        else:
            arrays.append(item)
            specs.append(pl.BlockSpec(memory_space=pltpu.VMEM))
    return pl.pallas_call(
        kernel,
        grid=(1,),
        in_specs=specs,
        out_specs=[pl.BlockSpec(memory_space=pltpu.VMEM)] * len(outs),
        out_shape=[jax.ShapeDtypeStruct(s, d) for s, d in outs],
        scratch_shapes=[pltpu.VMEM(s, d) for s, d in scratch],
        cost_estimate=pl.CostEstimate(flops=flops, transcendentals=1 << 19, bytes_accessed=4 << 20),
        compiler_params=pltpu.CompilerParams(vmem_limit_bytes=56 * 1024 * 1024),
    )(*arrays)


def dot(a, b, precision=None):
    return lax.dot_general(a, b, (((1,), (0,)), ((), ())), precision=precision, preferred_element_type=f32)


def dot_last(a, b, precision=None):
    return lax.dot_general(a, b, (((1,), (1,)), ((), ())), precision=precision, preferred_element_type=f32)


def dot_first(a, b, precision=None):
    return lax.dot_general(a, b, (((0,), (0,)), ((), ())), precision=precision, preferred_element_type=f32)


def thirds(x):
    first = x.astype(bf16)
    rest = x - first.astype(f32)
    second = rest.astype(bf16)
    return first, second, (rest - second.astype(f32)).astype(bf16)


def by_pieces(piece):
    def one(c, carry):
        piece(pl.ds(pl.multiple_of(c * PIECE, PIECE), PIECE))
        return carry

    lax.fori_loop(0, D // PIECE, one, 0)


def row_sums(x):
    ones = jnp.ones((8, x.shape[1]), bf16)
    return sum(dot_last(ones, part) for part in thirds(x))


def head_sums(x):
    picker = head_picker(x.shape[1])
    return sum(dot(part, picker) for part in thirds(x))


def ordered_sums(x, later):
    rows = x.shape[0]
    i = lax.broadcasted_iota(jnp.int32, (rows, rows), 0)
    j = lax.broadcasted_iota(jnp.int32, (rows, rows), 1)
    which = ((i <= j) if later else (i >= j)).astype(f32).astype(bf16)
    return sum(dot(which, part) for part in thirds(x))


def head_picker(rows):
    i = lax.broadcasted_iota(jnp.int32, (rows, LANES), 0)
    lane = lax.broadcasted_iota(jnp.int32, (rows, LANES), 1)
    return ((i >= lane * HEADDIM) & (i < (lane + 1) * HEADDIM)).astype(f32).astype(bf16)


def spread(ref, columns, rows, heads):
    for k in range(heads):
        ref[:, k * HEADDIM : (k + 1) * HEADDIM] = jnp.broadcast_to(columns[:, k : k + 1], (rows, HEADDIM))
    return ref[...]


def silu(x):
    return x * jax.nn.sigmoid(x)


def silu_and_grad(x):
    s = jax.nn.sigmoid(x)
    return x * s, s * (1.0 + x * (1.0 - s))


def document(place, position):
    start = jnp.int32(0)
    found = jnp.zeros(jnp.shape(position), jnp.int32) - 1
    for k in range(place.shape[0] - 3):
        found = found + jnp.where(position >= start, 1, 0)
        start = start + place[3 + k]
    return found


def marks_kernel(place, marks, ahead, seg_row):
    rows = marks.shape[0]
    position = lax.broadcasted_iota(jnp.int32, (rows, LANES), 0) + place[0]
    lane = lax.broadcasted_iota(jnp.int32, (rows, LANES), 1)
    own = document(place, position)
    age = position
    wide = lax.broadcasted_iota(jnp.int32, (rows + EDGE, LANES), 0) + (place[0] - EDGE)
    left = jnp.full((rows + EDGE, LANES), 1 << 30, jnp.int32)
    start = jnp.int32(0)
    for k in range(place.shape[0] - 3):
        age = jnp.where(position >= start, position - start, age)
        left = jnp.where((wide < start) & (start - wide < left), start - wide, left)
        start = start + place[3 + k]
    before = document(place, place[0] - 1)
    end = document(place, place[0] + rows - 1)
    found = (age >= lane).astype(f32)
    found = jnp.where(lane == 4, (own == before).astype(f32), found)
    found = jnp.where(lane == 5, (own == end).astype(f32), found)
    found = jnp.where(lane == 6, own.astype(f32), found)
    marks[...] = jnp.where(lane == 7, jnp.where(end == before, 1.0, 0.0).astype(f32), found)
    tap = lax.broadcasted_iota(jnp.int32, (rows + EDGE, LANES), 1)
    ahead[...] = (left > tap).astype(f32)
    seg_row[...] = document(place, lax.broadcasted_iota(jnp.int32, (8, rows), 1) + place[0]).astype(f32)


def pair_bias(marks, seg_row):
    rows = marks.shape[0]
    i = lax.broadcasted_iota(jnp.int32, (rows, rows), 0)
    j = lax.broadcasted_iota(jnp.int32, (rows, rows), 1)
    return jnp.where((i >= j) & (marks[:, 6:7] == seg_row[0:1, :]), 0.0, -1e30)


def pack(packed, state, decay):
    packed[: state.shape[0], :] = state
    packed[state.shape[0] :, :] = jnp.broadcast_to(decay, (EDGE, LANES))


def add_far(far, old, state_out):
    count = state_out.shape[0]
    if not far:
        state_out[...] = old[0][...]
        return
    for k in range(count // HEADDIM):
        at = slice(k * HEADDIM, (k + 1) * HEADDIM)
        state = far[0][at, :]
        if old:
            state = old[0][at, :] + jnp.broadcast_to(old[1][0:1, k : k + 1], (HEADDIM, STATE)) * state
        state_out[at, :] = state


def lane_row(ref, l, heads, scr):
    scr[...] = jnp.zeros(scr.shape, f32)
    scr[0:1, :heads] = ref[l : l + 1, :]
    return scr[0:1, :]


def state_kernel(marks_ref, x_ref, edge_ref, *refs, layer, heads, norm):
    if norm:
        gain, refs = refs[0], refs[1:]
    (value_w, state_w, step_w, filt_state, filt_value, state_bias, value_bias, step_bias, decay_log) = refs[:9]
    refs = refs[9:]
    if norm:
        normed_out, scale_out = refs[:2]
        refs = refs[2:]
    joined, filter_pre, active, step_pre, steps_out, cum_out, state_out, packed, tail_scr, lane_scr, row_scr = refs
    rows = x_ref.shape[0]
    marks = marks_ref[...]
    if norm:

        def normalise(raw):
            raw = raw.astype(f32)
            scale = lax.rsqrt(jnp.mean(raw * raw, axis=1, keepdims=True) + epsilon)
            return (raw * scale * gain[layer : layer + 1, :]).astype(bf16), scale

        x, scale = normalise(x_ref[...])
        e, _ = normalise(edge_ref[...])
        normed_out[...] = x
        scale_out[...] = jnp.broadcast_to(scale, scale_out.shape)
    else:
        x = x_ref[...]
        e = edge_ref[...]
    joined[EDGE:, : 2 * STATE] = dot(x, state_w[...])
    joined[EDGE:, 2 * STATE :] = dot(x, value_w[...])
    joined[:EDGE, : 2 * STATE] = dot(e, state_w[...])[EDGE:]
    joined[:EDGE, 2 * STATE :] = dot(e, value_w[...])[EDGE:]
    lane_scr[...] = jnp.zeros(lane_scr.shape, f32)
    lane_scr[:, :heads] = dot_last(x, step_w[...]) + step_bias[layer : layer + 1, :]
    for at, taps_w, bias in (
        (slice(0, 2 * STATE), filt_state, state_bias),
        (slice(2 * STATE, joined.shape[1]), filt_value, value_bias),
    ):
        pre = bias[layer : layer + 1, :] + taps_w[0:1, :] * joined[EDGE:, at]
        for k in range(1, CONV):
            pre = pre + taps_w[k : k + 1, :] * joined[EDGE - k : EDGE - k + rows, at] * marks[:, k : k + 1]
        filter_pre[:, at] = pre
        active[:, at] = silu(pre)
    b = active[:, :STATE]
    values = active[:, 2 * STATE :]
    pre_step = lane_scr[...]
    steps = jnp.maximum(pre_step, 0.0) + jnp.log1p(jnp.exp(-jnp.abs(pre_step)))
    rate = lane_row(decay_log, layer, heads, row_scr)
    cum = ordered_sums(steps * -jnp.exp(rate), False)
    step_pre[...] = pre_step
    steps_out[...] = steps
    cum_out[...] = cum
    last = cum[rows - 1 : rows, :]
    tail = jnp.exp(last - cum) * marks[:, 5:6] * steps
    state = dot_first(spread(tail_scr, tail, rows, heads) * values, b, high)
    state_out[...] = state
    pack(packed, state, jnp.exp(last) * marks[0:1, 7:8])


def local_kernel(
    marks, seg_row, normed, gate_w, active, steps, cum, skip, gate_pre, mixed_part, step_scr, *, layer, heads
):
    rows = normed.shape[0]
    half = rows // 2
    gate_pre[...] = dot(normed[...], gate_w[...])
    cum = cum[...]
    cum_t = cum.T
    step_scr[...] = spread(step_scr, steps[...], rows, heads) * active[:, 2 * STATE :]
    bias = pair_bias(marks[...], seg_row[...])
    for low, top in ((0, half), (half, rows)):
        here = bias[low:top, :top]
        scores = dot_last(active[low:top, STATE : 2 * STATE], active[:top, :STATE], high)
        for k in range(heads):
            at = slice(k * HEADDIM, (k + 1) * HEADDIM)
            source = slice(2 * STATE + k * HEADDIM, 2 * STATE + (k + 1) * HEADDIM)
            weights = scores * jnp.exp(cum[low:top, k : k + 1] - cum_t[k : k + 1, :top] + here)
            mixed_part[low:top, at] = (
                dot(weights, step_scr[:top, at], high) + skip[layer : layer + 1, k : k + 1] * active[low:top, source]
            )


def combine_kernel(place, *refs, span, sign, first):
    parts, refs = refs[:FAN], refs[FAN:]
    if not first:
        old, refs = refs[:2], refs[2:]
    state_out, decay_out, packed = refs
    count = state_out.shape[0]
    mine = lax.rem(lax.div(place[2], jnp.int32(span)), jnp.int32(FAN))

    def flag(condition):
        return jnp.where(condition, 1.0, 0.0).astype(f32)

    rows = [part[count : count + 1, :] for part in parts]
    chosen = [[flag((mine ^ r) == j) for j in range(FAN)] for r in range(FAN)]
    decay = [sum(chosen[r][j] * rows[r] for r in range(FAN)) for j in range(FAN)]
    order = range(FAN) if sign > 0 else range(FAN - 1, -1, -1)
    through = jnp.ones((1, LANES), f32)
    total = jnp.ones((1, LANES), f32)
    here = [None] * FAN
    whole = [None] * FAN
    for j in reversed(order):
        between = flag((mine - j) * sign > 0)
        here[j] = between * through
        whole[j] = total
        through = through * (between * decay[j] + (1.0 - between))
        total = total * decay[j]
    weight_here = [sum(chosen[r][j] * here[j] for j in range(FAN)) for r in range(FAN)]
    weight_whole = [sum(chosen[r][j] * whole[j] for j in range(FAN)) for r in range(FAN)]
    decay_out[...] = jnp.broadcast_to(through if first else old[1][0:1, :] * through, decay_out.shape)
    packed[count:, :] = jnp.broadcast_to(total, (EDGE, LANES))
    for k in range(count // HEADDIM):
        at = slice(k * HEADDIM, (k + 1) * HEADDIM)

        def wide(row):
            return jnp.broadcast_to(row[:, k : k + 1], (HEADDIM, STATE))

        values = [part[at, :] for part in parts]
        state = sum(wide(weight_here[r]) * values[r] for r in range(1, FAN))
        if not first:
            state = old[0][at, :] + wide(old[1][0:1, :]) * state
        state_out[at, :] = state
        packed[at, :] = sum(wide(weight_whole[r]) * values[r] for r in range(FAN))


def prefix(place, packed, sign, rows):
    count = lax.axis_size("seq")
    old = []
    span = 1
    while count // span > 2:
        parts = [packed] + [partner(packed, "seq", r * span) for r in range(1, FAN)]
        *old, packed = run(
            functools.partial(combine_kernel, span=span, sign=sign, first=not old),
            [place] + parts + old,
            [((rows, STATE), f32), ((EDGE, LANES), f32), ((rows + EDGE, STATE), f32)],
        )
        span *= FAN
    if count == span:
        return [], old
    return [shifted(packed, "seq", sign * span)], old


def gate_kernel(marks, mixed_part, active, gate_pre, cum, *refs, heads, fars):
    far, old = refs[:fars], refs[fars:-5]
    state_in, mixed_pre, gated, squares, scr = refs[-5:]
    rows = mixed_part.shape[0]
    add_far(far, old, state_in)
    carried = dot_last(active[:, STATE : 2 * STATE], state_in[...], high)
    entering = spread(scr, jnp.exp(cum[...]) * marks[:, 4:5], rows, heads)
    mixed = mixed_part[...] + entering * carried
    mixed_pre[...] = mixed
    out = mixed * silu(gate_pre[...])
    gated[...] = out
    squares[...] = row_sums(out * out)


def relative_blocks(place, scr, keep, give):
    size = keep.shape[1]
    for r in range(keep.shape[0]):
        keep[r] = scr[pl.ds(pl.multiple_of((place[1] ^ (2 * r)) * size, 8), size), :]
        give[r] = scr[pl.ds(pl.multiple_of((place[1] ^ (2 * r + 1)) * size, 8), size), :]


def out_kernel(place, gated, gain, out_w, *refs, layer):
    parts, (unit, scale_row, keep, give, scr) = refs[:-5], refs[-5:]
    total = parts[0][...]
    for part in parts[1:]:
        total = total + part[...]
    scale = lax.rsqrt(total / INNER + epsilon)
    scale_row[...] = scale
    column = scale.T[:, 0:1]
    rows = (gated[...] * column * gain[layer : layer + 1, :]).astype(bf16)
    unit[...] = rows
    scr[...] = dot(rows, out_w[...])
    relative_blocks(place, scr, keep, give)


def unit_kernel(grad_rows, out_w, gain, gated, unit_grad, inner, *, layer):
    grad = dot_last(grad_rows[...], out_w[...])
    unit_grad[...] = grad
    inner[...] = row_sums(gain[layer : layer + 1, :] * grad * gated[...])


def gated_kernel(
    marks, unit_grad, gated, gate_pre, mixed_pre, gain, scale_row, active, cum, *refs, heads, layer
):
    parts = refs[:-5]
    mixed_grad, gate_low, packed, row_out, scr = refs[-5:]
    rows = gated.shape[0]
    total = parts[0][...]
    for part in parts[1:]:
        total = total + part[...]
    scale = scale_row[...]
    cube = (scale * scale * scale * total / INNER).T[:, 0:1]
    column = scale.T[:, 0:1]
    grad = unit_grad[...]
    kept = gated[...]
    gated_grad = column * (gain[layer : layer + 1, :] * grad) - kept * cube
    level, slope = silu_and_grad(gate_pre[...])
    mixed = gated_grad * level
    mixed_grad[...] = mixed
    gate_low[...] = (gated_grad * mixed_pre[...] * slope).astype(bf16)
    row_out[...] = jnp.zeros(row_out.shape, f32)
    row_out[5:6, :] = jnp.sum(grad * kept * column, axis=0, keepdims=True)
    row_out[6:7, :] = jnp.sum(mixed * active[:, 2 * STATE :], axis=0, keepdims=True)
    cum = cum[...]
    entering = spread(scr, jnp.exp(cum) * marks[:, 4:5], rows, heads)
    state = dot_first(mixed * entering, active[:, STATE : 2 * STATE], high)
    pack(packed, state, jnp.exp(cum[rows - 1 : rows, :]) * marks[0:1, 7:8])


def scan_grad_kernel(
    marks_ref, seg_row, mixed_grad, active, mixed_pre, cum, steps, state_in, skip, grad_rows, unit, normed, gate_low,
    stepped_grad, b_grad, c_grad, out_dot, early, full_scr, step_scr, score_scr, *, heads, layer,
):
    rows = mixed_grad.shape[0]
    half = rows // 2
    inner = heads * HEADDIM
    marks = marks_ref[...]

    def piece(at):
        early[at, :inner] = dot_first(grad_rows[:, at], unit[...]).astype(bf16)
        early[at, inner:] = dot_first(normed[:, at], gate_low[...]).astype(bf16)

    by_pieces(piece)
    values = active[:, 2 * STATE :]
    cum = cum[...]
    cum_t = cum.T
    grad = mixed_grad[...]
    entering = spread(full_scr, jnp.exp(cum) * marks[:, 4:5], rows, heads)
    direct = dot(grad * entering, state_in[...], high)
    for k in range(heads):
        at = slice(k * HEADDIM, (k + 1) * HEADDIM)
        step_scr[0:1, at] = jnp.broadcast_to(skip[layer : layer + 1, k : k + 1], (1, HEADDIM))
    out_dot[...] = head_sums(grad * (mixed_pre[...] - step_scr[0:1, :] * values))
    step_scr[...] = spread(step_scr, steps[...], rows, heads) * values
    bias = pair_bias(marks, seg_row[...])
    score_scr[:half, half:] = jnp.zeros((half, rows - half), f32)
    for low, top in ((0, half), (half, rows)):
        here = bias[low:top, :top]
        scores = dot_last(active[low:top, STATE : 2 * STATE], active[:top, :STATE], high)
        score_grad = jnp.zeros((top - low, top), f32)
        for k in range(heads):
            at = slice(k * HEADDIM, (k + 1) * HEADDIM)
            decays = jnp.exp(cum[low:top, k : k + 1] - cum_t[k : k + 1, :top] + here)
            own = mixed_grad[low:top, at]
            score_grad = score_grad + decays * dot_last(own, step_scr[:top, at], high)
            found = dot_first(own, scores * decays, high).T
            if low == 0:
                stepped_grad[:top, at] = found
                stepped_grad[top:, at] = jnp.zeros((rows - top, HEADDIM), f32)
            else:
                stepped_grad[:, at] = stepped_grad[:, at] + found
        score_scr[low:top, :top] = score_grad
    total = score_scr[...]
    c_grad[...] = dot(total, active[:, :STATE], high) + direct
    b_grad[...] = dot_first(total, active[:, STATE : 2 * STATE], high)


def filter_grad_kernel(
    marks_ref, ahead, local_state, state_in, stepped_grad, b_grad, c_grad, out_dot, mixed_grad, filter_pre, active, joined, cum,
    steps, step_pre, decay_log, skip, filt_state, filt_value, row_in, *refs, heads, layer, fars,
):
    far, old = refs[:fars], refs[fars:-12]
    joined_grad, edge_out, step_low, row_out, shared_out = refs[-12:-7]
    tail_scr, step_scr, skip_scr, pad_scr, state_scr, later, lane_scr = refs[-7:]
    add_far(far, old, later)
    rows = mixed_grad.shape[0]
    marks = marks_ref[...]
    b = active[:, :STATE]
    values = active[:, 2 * STATE :]
    cum = cum[...]
    step = steps[...]
    last = cum[rows - 1 : rows, :]
    tail = jnp.exp(last - cum) * marks[:, 5:6]
    late = later[...]
    rate = -jnp.exp(lane_row(decay_log, layer, heads, lane_scr))
    tail_full = spread(tail_scr, tail, rows, heads)
    step_full = spread(step_scr, step, rows, heads)
    for k in range(heads):
        at = slice(k * HEADDIM, (k + 1) * HEADDIM)
        skip_scr[0:1, at] = jnp.broadcast_to(skip[layer : layer + 1, k : k + 1], (1, HEADDIM))
    total = stepped_grad[...] + tail_full * dot_last(b, late, high)
    value_grad = step_full * total + skip_scr[0:1, :] * mixed_grad[...]
    b_total = b_grad[...] + dot(tail_full * step_full * values, late, high)
    step_direct = head_sums(total * values)
    through = jnp.exp(last) * marks[0:1, 7:8]
    for k in range(heads):
        at = slice(k * HEADDIM, (k + 1) * HEADDIM)
        state_scr[at, :] = late[at, :] * (
            local_state[at, :] + jnp.broadcast_to(through[:, k : k + 1], (HEADDIM, STATE)) * state_in[at, :]
        )
    end = head_sums(row_sums(state_scr[...]))[0:1, :]
    log_grad = ordered_sums(out_dot[...] - step * step_direct, True) + end
    step_grad = (step_direct + rate * log_grad) * jax.nn.sigmoid(step_pre[...])
    step_low[...] = step_grad.astype(bf16)
    width = pad_scr.shape[1]
    pad_scr[:EDGE, :] = jnp.zeros((EDGE, width), f32)
    pad_scr[EDGE + rows :, :] = jnp.zeros((EDGE, width), f32)
    for at, grad in (
        (slice(0, STATE), b_total),
        (slice(STATE, 2 * STATE), c_grad[...]),
        (slice(2 * STATE, width), value_grad),
    ):
        pad_scr[EDGE : EDGE + rows, at] = grad * silu_and_grad(filter_pre[:, at])[1]
    shared_out[...] = jnp.zeros(shared_out.shape, f32)
    row_out[...] = row_in[...]
    for at, taps_w, out in (
        (slice(0, 2 * STATE), filt_state, shared_out.at[:, : 2 * STATE]),
        (slice(2 * STATE, width), filt_value, row_out),
    ):
        grad = taps_w[0:1, :] * pad_scr[: EDGE + rows, at]
        for k in range(1, CONV):
            grad = grad + taps_w[k : k + 1, :] * pad_scr[k : k + EDGE + rows, at] * ahead[:, k : k + 1]
        joined_grad[:, at] = grad[EDGE:]
        edge_out[:, at] = grad[:EDGE]
        own = pad_scr[EDGE : EDGE + rows, at]
        for k in range(CONV):
            masked = own * joined[EDGE - k : EDGE - k + rows, at]
            if k > 0:
                masked = masked * marks[:, k : k + 1]
            out[k : k + 1, :] = jnp.sum(masked, axis=0, keepdims=True)
        out[4:5, :] = jnp.sum(own, axis=0, keepdims=True)
    row_out[7:8, :heads] = jnp.sum(step_grad, axis=0, keepdims=True)[:, :heads]
    row_out[7:8, HEADDIM : HEADDIM + heads] = (jnp.sum(step * log_grad, axis=0, keepdims=True) * rate)[:, :heads]


def normed_grad_kernel(
    place, joined_grad, edge_grad, gate_low, step_low, gate_w, value_w, state_w, step_w, shared_in, *refs, heads, last
):
    rows = joined_grad.shape[0]
    shared_out, keep, give, value_low, state_keep, state_give, scr, part_scr = refs[-8:]
    scr[...] = joined_grad[...]
    scr[rows - EDGE :, :] = scr[rows - EDGE :, :] + edge_grad[...]
    low = scr[:, 2 * STATE :].astype(bf16)
    value_low[...] = low
    size = state_keep.shape[2]
    for k in range(2 * STATE // size):
        relative = place[1] ^ k

        @pl.when((relative & 1) == 0)
        def _():
            state_keep[relative >> 1] = scr[:, k * size : (k + 1) * size]

        @pl.when((relative & 1) == 1)
        def _():
            state_give[relative >> 1] = scr[:, k * size : (k + 1) * size]

    part = (
        dot_last(gate_low[...], gate_w[...])
        + dot_last(low, value_w[...])
        + dot(step_low[:, :heads], step_w[...])
        + sum(dot_last(third, state_w[...]) for third in thirds(scr[:, : 2 * STATE]))
    )
    part_scr[...] = part
    relative_blocks(place, part_scr, keep, give)
    shared_out[...] = shared_in[...]
    if last:
        tokens, scale = refs[:2]
        norm_rows = tokens[...].astype(f32) * scale[:, 0:1]
        shared_out[5:6, :] = jnp.sum(part * norm_rows, axis=0, keepdims=True)


def late_kernel(normed, value_low, step_low, state_a, state_b, late, *scrs):
    inner = value_low.shape[1]
    size = state_a.shape[1]
    for scr, third in zip(scrs, thirds(state_a[...] + state_b[...])):
        scr[...] = third

    def piece(at):
        x = normed[:, at]
        late[at, :inner] = dot_first(x, value_low[...]).astype(bf16)
        state = sum(dot_first(x, scr[...]) for scr in scrs)
        late[at, inner : inner + size] = state.astype(bf16)
        late[at, inner + size :] = dot_first(x, step_low[...]).astype(bf16)

    by_pieces(piece)


def step(
    tokens,
    cotangent,
    doc_lengths,
    norm_gain,
    gate_proj,
    value_proj,
    state_proj,
    step_proj,
    step_bias,
    decay_log,
    skip_gain,
    filter_value,
    filter_value_bias,
    filter_state,
    filter_state_bias,
    gated_gain,
    out_proj,
):
    rows = tokens.shape[0]
    head_count = lax.axis_size("head")
    seq_count = lax.axis_size("seq")
    me = lax.axis_index("head")
    inner = gate_proj.shape[2]
    heads = step_proj.shape[2]
    width = 2 * STATE + inner
    share = D // head_count
    part_rows = rows // head_count
    state_share = 2 * STATE // head_count
    half = head_count // 2

    def own_rows(matrix):
        return lax.dynamic_slice_in_dim(matrix, me * part_rows, part_rows, 0)

    at_seq = lax.axis_index("seq")
    numbers = jnp.concatenate(
        [jnp.stack([at_seq * rows, me, at_seq]).astype(jnp.int32), doc_lengths.astype(jnp.int32)]
    )
    place = (numbers, SMEM)
    step_rows = jnp.swapaxes(step_proj, 1, 2)
    marks, marks_ahead, seg_row = run(
        marks_kernel, [place], [((rows, LANES), f32), ((rows + EDGE, LANES), f32), ((8, rows), f32)]
    )

    kept = []
    stream_rows = own_rows(tokens).astype(f32)
    normed = None
    normed_rows = None
    scale_rows = None
    for l in range(LAYERS):
        source = tokens if l == 0 else normed
        edge = shifted(source[rows - 2 * EDGE :], "seq", 1)
        norm_outs = [((rows, D), bf16), ((rows, LANES), f32)] if l == 0 else []
        found = run(
            functools.partial(state_kernel, layer=l, heads=heads, norm=l == 0),
            [marks, source, edge]
            + ([norm_gain] if l == 0 else [])
            + [
                (value_proj, l),
                (state_proj, l),
                (step_rows, l),
                (filter_state, l),
                (filter_value, l),
                filter_state_bias,
                filter_value_bias,
                step_bias,
                decay_log,
            ],
            norm_outs
            + [
                ((rows + EDGE, width), f32),
                ((rows, width), f32),
                ((rows, width), f32),
                ((rows, LANES), f32),
                ((rows, LANES), f32),
                ((rows, LANES), f32),
                ((inner, STATE), f32),
                ((inner + EDGE, STATE), f32),
            ],
            [((rows, inner), f32), ((rows, LANES), f32), ((8, LANES), f32)],
        )
        scale_full = None
        if l == 0:
            normed, scale_full = found[:2]
            found = found[2:]
            normed_rows = own_rows(normed)
            scale_rows = own_rows(scale_full)[:, 0]
        joined, filter_pre, active, step_pre, steps, cum, local_state, packed = found
        gate_pre, mixed_part = run(
            functools.partial(local_kernel, layer=l, heads=heads),
            [marks, seg_row, normed, (gate_proj, l), active, steps, cum, skip_gain],
            [((rows, inner), f32), ((rows, inner), f32)],
            [((rows, inner), f32)],
        )
        far, old = prefix(place, packed, 1, inner)
        state_in, mixed_pre, gated, squares = run(
            functools.partial(gate_kernel, heads=heads, fars=len(far)),
            [marks, mixed_part, active, gate_pre, cum, *far, *old],
            [((inner, STATE), f32), ((rows, inner), f32), ((rows, inner), f32), ((8, rows), f32)],
            [((rows, inner), f32)],
        )
        square_parts = copies_over(squares, "head")
        unit, scale_row, keep, give = run(
            functools.partial(out_kernel, layer=l),
            [place, gated, gated_gain, (out_proj, l), *square_parts],
            [
                ((rows, inner), bf16),
                ((8, rows), f32),
                ((half, part_rows, D), f32),
                ((half, part_rows, D), f32),
            ],
            [((rows, D), f32)],
        )
        kept.append(
            SimpleNamespace(
                normed=normed, gate_pre=gate_pre, joined=joined, filter_pre=filter_pre, active=active, local_state=local_state,
                step_pre=step_pre, steps=steps, cum=cum, state_in=state_in, mixed_pre=mixed_pre, gated=gated,
                scale_row=scale_row, unit=unit, stream_rows=stream_rows, normed_rows=normed_rows,
                scale_rows=scale_rows, scale_full=scale_full,
            )
        )
        stream_rows = stream_rows + sum(scatter_relative(keep, give, "head"))
        if l < LAYERS - 1:
            scale_rows = lax.rsqrt(jnp.mean(stream_rows * stream_rows, axis=1) + epsilon)
            normed_rows = (stream_rows * scale_rows[:, None] * norm_gain[l + 1][None, :]).astype(bf16)
            normed = lax.all_gather(normed_rows, "head", axis=0, tiled=True)

    def pieces_sum(matrix):
        blocks = matrix.reshape(seq_count, D // seq_count, matrix.shape[1])
        got = lax.all_to_all(blocks, "seq", 0, 0, tiled=True)
        return jnp.sum(got.astype(f32), axis=0)

    early = [None] * LAYERS
    late = [None] * LAYERS
    local_rows = [None] * LAYERS
    shared_rows = [None] * LAYERS
    residual_rows = own_rows(cotangent)
    grad_rows = cotangent.astype(bf16)
    for l in reversed(range(LAYERS)):
        k = kept[l]
        unit_grad, inner_sum = run(
            functools.partial(unit_kernel, layer=l),
            [grad_rows, (out_proj, l), gated_gain, k.gated],
            [((rows, inner), f32), ((8, rows), f32)],
        )
        inner_parts = copies_over(inner_sum, "head")
        mixed_grad, gate_low, grad_packed, gain_rows = run(
            functools.partial(gated_kernel, heads=heads, layer=l),
            [
                marks, unit_grad, k.gated, k.gate_pre, k.mixed_pre, gated_gain, k.scale_row,
                k.active, k.cum, *inner_parts,
            ],
            [
                ((rows, inner), f32),
                ((rows, inner), bf16),
                ((inner + EDGE, STATE), f32),
                ((8, inner), f32),
            ],
            [((rows, inner), f32)],
        )
        stepped_grad, b_grad, c_grad, out_dot, early_part = run(
            functools.partial(scan_grad_kernel, heads=heads, layer=l),
            [
                marks, seg_row, mixed_grad, k.active, k.mixed_pre, k.cum, k.steps, k.state_in, skip_gain,
                grad_rows, k.unit, k.normed, gate_low,
            ],
            [
                ((rows, inner), f32),
                ((rows, STATE), f32),
                ((rows, STATE), f32),
                ((rows, LANES), f32),
                ((D, 2 * inner), bf16),
            ],
            [((rows, inner), f32), ((rows, inner), f32), ((rows, rows), f32)],
        )
        early[l] = pieces_sum(early_part)
        far, old = prefix(place, grad_packed, -1, inner)
        joined_grad, edge_out, step_low, local_rows[l], shared = run(
            functools.partial(filter_grad_kernel, heads=heads, layer=l, fars=len(far)),
            [
                marks, marks_ahead, k.local_state, k.state_in, stepped_grad, b_grad, c_grad, out_dot,
                mixed_grad, k.filter_pre, k.active, k.joined, k.cum, k.steps, k.step_pre, decay_log, skip_gain,
                (filter_state, l), (filter_value, l), gain_rows, *far, *old,
            ],
            [
                ((rows, width), f32),
                ((EDGE, width), f32),
                ((rows, LANES), bf16),
                ((8, inner), f32),
                ((8, D), f32),
            ],
            [
                ((rows, inner), f32),
                ((rows, inner), f32),
                ((8, inner), f32),
                ((rows + 2 * EDGE, width), f32),
                ((inner, STATE), f32),
                ((inner, STATE), f32),
                ((8, LANES), f32),
            ],
        )
        edge_grad = shifted(edge_out, "seq", -1)
        last = l == 0
        shared_rows[l], keep, give, value_low, state_keep, state_give = run(
            functools.partial(normed_grad_kernel, heads=heads, last=last),
            [
                place, joined_grad, edge_grad, gate_low, step_low, (gate_proj, l), (value_proj, l), (state_proj, l),
                (step_rows, l), shared,
            ]
            + ([tokens, k.scale_full] if last else []),
            [
                ((8, D), f32),
                ((half, part_rows, D), f32),
                ((half, part_rows, D), f32),
                ((rows, inner), bf16),
                ((half, rows, state_share), f32),
                ((half, rows, state_share), f32),
            ],
            [((rows, width), f32), ((rows, D), f32)],
        )
        total = sum(scatter_relative(keep, give, "head"))
        state_parts = scatter_relative(state_keep, state_give, "head")
        mean_dot = jnp.mean(k.normed_rows.astype(f32) * total, axis=1)
        norm_rows = k.stream_rows * k.scale_rows[:, None]
        residual_rows = residual_rows + k.scale_rows[:, None] * (
            norm_gain[l][None, :] * total - norm_rows * mean_dot[:, None]
        )
        if not last:
            grad_rows = lax.all_gather(residual_rows.astype(bf16), "head", axis=0, tiled=True)
            fifth = (jnp.arange(8) == 5).astype(f32)
            shared_rows[l] = shared_rows[l] + fifth[:, None] * jnp.sum(total * norm_rows, axis=0)[None, :]
        (late_part,) = run(
            late_kernel,
            [k.normed, value_low, step_low, *state_parts],
            [((D, inner + state_share + LANES), bf16)],
            [((rows, state_share), bf16)] * 3,
        )
        late[l] = pieces_sum(late_part)

    pairs = jnp.concatenate(
        [
            stream_rows.reshape(part_rows, head_count, share),
            residual_rows.reshape(part_rows, head_count, share),
        ],
        axis=2,
    )
    got = [lax.dynamic_index_in_dim(pairs, me ^ r, 1, keepdims=False) for r in range(head_count)]
    got = [got[0]] + [partner(got[r], "head", r) for r in range(1, head_count)]
    placed = jnp.zeros((head_count, part_rows, 2 * share), f32)
    for r in range(head_count):
        placed = lax.dynamic_update_index_in_dim(placed, got[r], me ^ r, 0)
    placed = placed.reshape(rows, 2 * share)
    mixed = placed[:, :share].astype(bf16)
    residual_columns = placed[:, share:]

    shared = functools.reduce(jnp.add, copies_over(jnp.concatenate(shared_rows, axis=0), "head"))
    small = butterfly_sum(jnp.concatenate([shared, jnp.concatenate(local_rows, axis=0)], axis=1), "seq")
    shared = small[:, :D].reshape(LAYERS, 8, D)
    own = small[:, D:].reshape(LAYERS, 8, inner)
    filter_share = lax.dynamic_slice_in_dim(shared, me * state_share, state_share, 2)

    def both(pick):
        return jnp.stack([pick(l) for l in range(LAYERS)], axis=0)

    return (
        mixed,
        residual_columns,
        lax.dynamic_slice_in_dim(shared[:, 5], me * share, share, 1),
        both(lambda l: early[l][:, inner:]),
        both(lambda l: late[l][:, :inner]),
        both(lambda l: late[l][:, inner : inner + state_share]),
        both(lambda l: late[l][:, inner + state_share : inner + state_share + heads]),
        own[:, 7, :heads],
        own[:, 7, HEADDIM : HEADDIM + heads],
        jnp.sum(own[:, 6].reshape(LAYERS, heads, HEADDIM), axis=2),
        own[:, :CONV],
        own[:, CONV],
        filter_share[:, :CONV],
        filter_share[:, CONV],
        own[:, 5],
        both(lambda l: early[l][:, :inner].T),
    )


def solution(mesh):
    placed = (
        P("seq", None),
        P("seq", None),
        P(),
        P(),
        P(None, None, "head"),
        P(None, None, "head"),
        P(),
        P(None, None, "head"),
        P(None, "head"),
        P(None, "head"),
        P(None, "head"),
        P(None, None, "head"),
        P(None, "head"),
        P(),
        P(),
        P(None, "head"),
        P(None, "head", None),
    )
    return jax.shard_map(
        step,
        mesh=mesh,
        in_specs=placed,
        out_specs=(
            P("seq", "head"),
            P("seq", "head"),
            P(None, "head"),
            P(None, "seq", "head"),
            P(None, "seq", "head"),
            P(None, "seq", "head"),
            P(None, "seq", "head"),
            P(None, "head"),
            P(None, "head"),
            P(None, "head"),
            P(None, None, "head"),
            P(None, "head"),
            P(None, None, "head"),
            P(None, "head"),
            P(None, "head"),
            P(None, "head", "seq"),
        ),
        check_vma=False,
    )
```
